128 devices in a mesh: group: 4 (over y_hi, core), pair: 32 (over x, z, y_lo).
Axes of the slice: x: 4, y: 4 (y_hi: 2, y_lo: 2; y = y_hi * 2 + y_lo), z: 4, core: 2. Of those that a mesh axis runs over, the one named last changes fastest.
Arguments:
- genotypes: int32 [4096, 65536], P(None, ('group', 'pair')), may hold values from 0 to 2, as said below
- dest_group: int32 [256], replicated, may hold values from 0 to 3, as said below
Outputs:
- rotated: bfloat16 [4096, 65536], P(None, ('group', 'pair'))
The draws below stay inside these ranges and needn't reach their ends.
Inputs may be any that keep to these rules, and one draw needn't show every extreme that they name: For every pair index p and side k there is an offset s with dest_group[(g * 32 + p) * 2 + k] = (g + s) mod 4 for all g, and the two sides have different offsets; so every position (t, p, k) receives exactly one block. `genotypes`: allele counts of two alleles.
All inputs are finite; a program needn't handle non-finite values.
Results may differ from the reference program's by a relative error of at most 0.0077.
Values may be sent and summed in bfloat16 or wider, within the bound.
A program may use at most 128 MiB of HBM per device.

```python
import jax
import jax.numpy as jnp
from jax import lax

INDIV = 4096
BLOCK = 256
ROUNDS = 3
GROUPS = 4
PAIRS = 32
NBLK = 256
NSNP = 65536


def draw_haplotype(key, indiv_freq):
    key_fresh = jax.random.fold_in(key, 1)
    key_switch = jax.random.fold_in(key, 2)
    fresh = jax.random.randint(key_fresh, (INDIV, NSNP), 0, 1000)
    switch = jax.random.randint(key_switch, (INDIV, NSNP), 0, 1000) < 400
    snp_iota = lax.broadcasted_iota(jnp.int32, (INDIV, NSNP), 1)
    marks = jnp.where(switch, snp_iota, 0).astype(jnp.int32)
    source = lax.cummax(marks, axis=1).astype(jnp.int32)
    copied = jnp.take_along_axis(fresh, source, axis=1)
    return (copied < indiv_freq).astype(jnp.int32)


def draw_genotypes(key, part):
    key_freq = jax.random.fold_in(key, 11)
    key_shift = jax.random.fold_in(key, 12)
    key_ancestry = jax.random.fold_in(key, 13)
    key_first = jax.random.fold_in(key, 14)
    key_second = jax.random.fold_in(key, 15)
    base_level = jax.random.randint(key_freq, (1, NSNP), 100, 901)
    pop_shift = jax.random.randint(key_shift, (4, NSNP), -150, 151)
    pop_freq = jnp.clip(base_level + pop_shift, 20, 980).astype(jnp.int32)
    ancestry = jax.random.randint(key_ancestry, (INDIV,), 0, 4).astype(jnp.int32)
    indiv_freq = pop_freq[ancestry]
    first_allele = draw_haplotype(key_first, indiv_freq)
    second_allele = draw_haplotype(key_second, indiv_freq)
    return (first_allele + second_allele).astype(jnp.int32)


def draw_dest_group(key, part):
    key_side0 = jax.random.fold_in(key, 21)
    key_side1 = jax.random.fold_in(key, 22)
    offset_zero = jax.random.randint(key_side0, (PAIRS,), 0, GROUPS)
    offset_one = (offset_zero + jax.random.randint(key_side1, (PAIRS,), 1, GROUPS)) % GROUPS
    groups_iota = jnp.arange(GROUPS, dtype=jnp.int32)[:, None]
    dest_zero = (groups_iota + offset_zero[None, :]) % GROUPS
    dest_one = (groups_iota + offset_one[None, :]) % GROUPS
    return jnp.stack([dest_zero, dest_one], axis=-1).reshape(NBLK).astype(jnp.int32)


def setup_inputs(seed: int = 0) -> dict:
    streams_of = jax.random.split(jax.random.key(seed), 3)
    genotypes = draw_genotypes(jax.random.fold_in(streams_of[2], 71), 0)
    dest_group = draw_dest_group(jax.random.fold_in(streams_of[2], 71), 0)
    return {"genotypes": genotypes, "dest_group": dest_group}


epsilon = 1e-05

def standardize(counts):
    values = counts.astype(jnp.float32)
    col_mean = lax.optimization_barrier(jnp.mean(values, axis=0))
    centred = values - col_mean
    col_var = lax.optimization_barrier(jnp.mean(centred * centred, axis=0))
    return (centred / jnp.sqrt(col_var + epsilon)).astype(jnp.bfloat16)

def rotation_for(top_block, low_block):
    blk_width = top_block.shape[1]
    top_wide = top_block.astype(jnp.float32)
    low_wide = low_block.astype(jnp.float32)
    norm_top = lax.optimization_barrier(jnp.sum(top_wide * top_wide, axis=0))
    norm_low = lax.optimization_barrier(jnp.sum(low_wide * low_wide, axis=0))
    cross_gram = lax.dot_general(top_block.astype(jnp.float32), low_block.astype(jnp.float32), (((0,), (0,)), ((), ())), preferred_element_type=jnp.float32)
    coupling = 2.0 * cross_gram / (norm_top[:, None] + norm_low[None, :] + epsilon)
    zero_block = jnp.zeros((blk_width, blk_width), jnp.float32)
    skew_part = jnp.concatenate([jnp.concatenate([zero_block, coupling], axis=1), jnp.concatenate([-coupling.T, zero_block], axis=1)], axis=0)
    identity = jnp.eye(2 * blk_width, dtype=jnp.float32)
    gram_matrix = identity + jnp.dot(skew_part.T, skew_part, precision=lax.Precision.HIGHEST)
    factor = jnp.linalg.cholesky(gram_matrix)
    lifted = identity + skew_part
    rotation = jax.scipy.linalg.solve_triangular(factor, lifted.T, lower=True).T
    return rotation.astype(jnp.bfloat16)

def apply_pair(top_block, low_block):
    rotation = rotation_for(top_block, low_block)
    joined = jnp.concatenate([top_block, low_block], axis=1)
    result = jnp.dot(joined.astype(jnp.float32), rotation.astype(jnp.float32), preferred_element_type=jnp.float32).astype(jnp.bfloat16)
    return (result[:, :BLOCK], result[:, BLOCK:])

def reference(genotypes, dest_group):
    counts = genotypes.reshape(INDIV, GROUPS, PAIRS * 2 * BLOCK)
    counts = jnp.moveaxis(counts, 1, 0)
    scaled = lax.map(standardize, counts)
    scaled = scaled.reshape(GROUPS, INDIV, PAIRS, 2, BLOCK)
    scaled = jnp.transpose(scaled, (0, 2, 3, 1, 4))
    dest_table = dest_group.reshape(GROUPS, PAIRS, 2)
    groups_iota = jnp.arange(GROUPS, dtype=jnp.int32)
    matches = (dest_table[None, :, :, :] == groups_iota[:, None, None, None]).astype(jnp.int32)
    source = lax.optimization_barrier(jnp.sum(matches * groups_iota[None, :, None, None], axis=1)).astype(jnp.int32)
    pair_iota = jnp.arange(PAIRS, dtype=jnp.int32)[None, :, None]
    side_iota = jnp.arange(2, dtype=jnp.int32)[None, None, :]
    placed = scaled[source, pair_iota, side_iota]
    top_all = placed[:, :, 0]
    low_all = placed[:, :, 1]
    group_step = jax.vmap(apply_pair)
    for cycle_round in range(ROUNDS):
        top_all, low_new = lax.map(lambda pieces: group_step(pieces[0], pieces[1]), (top_all, low_all))
        low_all = jnp.roll(low_new, 1, axis=1)
    final = jnp.stack([top_all, low_all], axis=2)
    final = jnp.transpose(final, (3, 0, 1, 2, 4))
    return final.reshape(INDIV, NSNP)
```

```python
import jax
import jax.numpy as jnp
from jax import lax
from jax.experimental import pallas as pl
from jax.experimental.pallas import tpu as pltpu
from jax.sharding import PartitionSpec as P

ROUNDS = 3
HALF = 64
CHUNK = 512

epsilon = 1e-05


def passed_along(array, axis, by):
    size = lax.axis_size(axis)
    return lax.ppermute(array, axis, [(i, (i + by) % size) for i in range(size)])


def standardize(counts):
    values = counts.astype(jnp.float32)
    col_mean = jnp.mean(values, axis=0)
    centred = values - col_mean
    col_var = jnp.mean(centred * centred, axis=0)
    return (centred / jnp.sqrt(col_var + epsilon)).astype(jnp.bfloat16)


def product(left, right, left_dim, right_dim):
    dims = (((left_dim,), (right_dim,)), ((), ()))
    return lax.dot_general(
        left, right, dims, precision=lax.Precision.HIGHEST, preferred_element_type=jnp.float32
    )


def inverse_factor_pair(rows):
    lane = lax.broadcasted_iota(jnp.int32, (8, 128), 1)
    sub = lax.broadcasted_iota(jnp.int32, (8, 128), 0)
    start = jnp.where(lane < HALF, 0, HALF)
    col = lane - start
    rows = list(rows)
    for j in range(HALF):
        tile, s = divmod(j, 8)
        index = start + j
        here = col == j
        pivot_row = jnp.broadcast_to(rows[tile][s : s + 1, :], (8, 128))
        inverse = 1.0 / jnp.take_along_axis(pivot_row, index, axis=1)
        scaled = jnp.where(here, 1.0, pivot_row) * inverse
        for r in range(tile if s < 7 else tile + 1, 8):
            ratio = jnp.take_along_axis(rows[r], index, axis=1)
            update = jnp.where(here, 0.0, rows[r]) - ratio * scaled
            rows[r] = jnp.where(sub > s, update, rows[r]) if r == tile else update
    done = []
    for r in range(8):
        row = sub + 8 * r
        scale = lax.rsqrt(jnp.take_along_axis(rows[r], start + row, axis=1))
        done.append(jnp.where(col < row, rows[r] * scale, jnp.where(col == row, scale, 0.0)))
    return jnp.concatenate(done, axis=0)


def invert_factors(gram):
    width = gram.shape[1]
    eye_row = lax.broadcasted_iota(jnp.int32, (HALF, HALF), 0)
    eye = (eye_row == lax.broadcasted_iota(jnp.int32, (HALF, HALF), 1)).astype(jnp.float32)
    lanes = lax.broadcasted_iota(jnp.int32, (HALF, width), 1)
    for low in range(0, width, HALF):
        high = low + HALF
        block = jnp.concatenate([gram[m, low:high, low:high] for m in range(2)], axis=1)
        both = inverse_factor_pair([block[8 * r : 8 * r + 8] for r in range(8)])
        for m in range(2):
            gram[m, low:high, low:high] = eye
            panel = product(both[:, HALF * m : HALF * m + HALF], gram[m, low:high, :], 1, 0)
            if high < width:
                gram[m, high:, low:high] = jnp.zeros((width - high, HALF), jnp.float32)
                gram[m, high:, :] = gram[m, high:, :] - product(panel[:, high:], panel, 0, 0)
                panel = jnp.where(lanes < high, panel, 0.0)
            gram[m, low:high, :] = panel


def rotate_kernel(top_ref, low_ref, new_top_ref, new_low_ref, gram, cross, norm, turn):
    rows, width = top_ref.shape
    cross[...] = jnp.zeros_like(cross)
    norm[...] = jnp.zeros_like(norm)

    @pl.loop(0, rows // CHUNK)
    def _(i):
        part = pl.ds(pl.multiple_of(i * CHUNK, CHUNK), CHUNK)
        top, low = top_ref[part, :], low_ref[part, :]
        cross[...] += lax.dot_general(
            top, low, (((0,), (0,)), ((), ())), preferred_element_type=jnp.float32
        )
        for m, block in enumerate((top, low)):
            wide = block.astype(jnp.float32)
            norm[m] += jnp.sum((wide * wide).reshape(CHUNK // 8, 8, width), axis=0)

    norm_top = jnp.broadcast_to(jnp.sum(norm[0], axis=0, keepdims=True), (width, width)).T
    norm_low = jnp.sum(norm[1], axis=0, keepdims=True)
    coupling = 2.0 * cross[...] / (norm_top + norm_low + epsilon)
    cross[...] = coupling
    row = lax.broadcasted_iota(jnp.int32, (width, width), 0)
    eye = (row == lax.broadcasted_iota(jnp.int32, (width, width), 1)).astype(jnp.float32)
    gram[0] = eye + product(coupling, coupling, 1, 1)
    gram[1] = eye + product(coupling, coupling, 0, 0)
    invert_factors(gram)
    turn[0:width, 0:width] = gram[0].T.astype(jnp.bfloat16)
    turn[0:width, width:] = product(cross[...], gram[1], 1, 1).astype(jnp.bfloat16)
    turn[width:, 0:width] = (-product(cross[...], gram[0], 0, 1)).astype(jnp.bfloat16)
    turn[width:, width:] = gram[1].T.astype(jnp.bfloat16)

    @pl.loop(0, rows // CHUNK)
    def _(i):
        part = pl.ds(pl.multiple_of(i * CHUNK, CHUNK), CHUNK)
        joined = jnp.concatenate([top_ref[part, :], low_ref[part, :]], axis=1)
        result = jnp.dot(joined, turn[...], preferred_element_type=jnp.float32).astype(jnp.bfloat16)
        new_top_ref[part, :] = result[:, :width]
        new_low_ref[part, :] = result[:, width:]


def rotate(top, low):
    width = top.shape[1]
    vmem = pl.BlockSpec(memory_space=pltpu.VMEM)
    return pl.pallas_call(
        rotate_kernel,
        out_shape=[jax.ShapeDtypeStruct(top.shape, top.dtype)] * 2,
        in_specs=[vmem, vmem],
        out_specs=[vmem, vmem],
        scratch_shapes=[
            pltpu.VMEM((2, width, width), jnp.float32),
            pltpu.VMEM((width, width), jnp.float32),
            pltpu.VMEM((2, 8, width), jnp.float32),
            pltpu.VMEM((2 * width, 2 * width), jnp.bfloat16),
        ],
        compiler_params=pltpu.CompilerParams(vmem_limit_bytes=32 * 2**20),
    )(top, low)


def body(genotypes, dest_group):
    num_groups = lax.axis_size("group")
    num_pairs = lax.axis_size("pair")
    own_group = lax.axis_index("group")
    own_pair = lax.axis_index("pair")
    blk_width = genotypes.shape[1] // 2
    scaled = standardize(genotypes)
    first_block = scaled[:, :blk_width]
    second_block = scaled[:, blk_width:]
    dest_table = dest_group.reshape(num_groups, num_pairs, 2)
    column = lax.dynamic_index_in_dim(dest_table, own_pair, 1, keepdims=False)
    own_dest = lax.dynamic_index_in_dim(column, own_group, 0, keepdims=False)
    groups_iota = jnp.arange(num_groups, dtype=jnp.int32)
    source_zero = jnp.sum(jnp.where(column[:, 0] == own_group, groups_iota, 0))
    source_one = jnp.sum(jnp.where(column[:, 1] == own_group, groups_iota, 0))
    pick_zero = (groups_iota == own_dest[0])[:, None, None]
    pick_one = (groups_iota == own_dest[1])[:, None, None]
    send_slots = jnp.where(
        pick_zero,
        first_block[None],
        jnp.where(pick_one, second_block[None], jnp.zeros_like(first_block)[None]),
    )
    arrived = lax.all_to_all(send_slots, "group", split_axis=0, concat_axis=0, tiled=True)
    top_block = lax.dynamic_index_in_dim(arrived, source_zero, 0, keepdims=False)
    low_block = lax.dynamic_index_in_dim(arrived, source_one, 0, keepdims=False)
    for cycle_round in range(ROUNDS):
        top_block, low_block = rotate(top_block, low_block)
        low_block = passed_along(low_block, "pair", 1)
    return jnp.concatenate([top_block, low_block], axis=1)


def solution(mesh):
    in_specs = (P(None, ("group", "pair")), P())
    out_specs = P(None, ("group", "pair"))
    return jax.shard_map(body, mesh=mesh, in_specs=in_specs, out_specs=out_specs, check_vma=False)
```

```python
import jax
import jax.numpy as jnp
from jax import lax
from jax.experimental import pallas as pl
from jax.experimental.pallas import tpu as pltpu
from jax.sharding import PartitionSpec as P

ROUNDS = 3
HALF = 64
CHUNK = 512

epsilon = 1e-05


def standardize(counts):
    values = counts.astype(jnp.float32)
    col_mean = jnp.mean(values, axis=0)
    centred = values - col_mean
    col_var = jnp.mean(centred * centred, axis=0)
    return (centred / jnp.sqrt(col_var + epsilon)).astype(jnp.bfloat16)


def product(left, right, left_dim, right_dim):
    dims = (((left_dim,), (right_dim,)), ((), ()))
    return lax.dot_general(
        left, right, dims, precision=lax.Precision.HIGHEST, preferred_element_type=jnp.float32
    )


def spread(tile, row):
    return jnp.broadcast_to(tile[row : row + 1, :], tile.shape)


def inverse_factor_pair(rows):
    lane = lax.broadcasted_iota(jnp.int32, (8, 128), 1)
    sub = lax.broadcasted_iota(jnp.int32, (8, 128), 0)
    start = jnp.where(lane < HALF, 0, HALF)
    col = lane - start
    rows = list(rows)
    pivots = [jnp.ones((8, 128), jnp.float32)] * 8
    for first in range(0, HALF, 8):
        tile = first // 8
        cols = [
            [jnp.take_along_axis(rows[r], start + (first + m), axis=1) for r in range(tile, 8)]
            for m in range(8)
        ]
        for m in range(8):
            here = col == first + m
            pivot = spread(cols[m][0], m)
            inverse = 1.0 / pivot
            pivots[tile] = jnp.where(sub == m, pivot, pivots[tile])
            cols[m][0] = jnp.where(sub > m, cols[m][0], 0.0)
            for n in range(m + 1, 8):
                ratio = spread(cols[n][0], m) * inverse
                cols[n] = [c - f * ratio for c, f in zip(cols[n], cols[m])]
            scaled = jnp.where(here, 1.0, spread(rows[tile], m)) * inverse
            for r in range(tile, 8):
                rows[r] = jnp.where(here, 0.0, rows[r]) - cols[m][r - tile] * scaled
    done = []
    for r in range(8):
        row = sub + 8 * r
        scale = lax.rsqrt(pivots[r])
        done.append(jnp.where(col < row, rows[r] * scale, jnp.where(col == row, scale, 0.0)))
    return jnp.concatenate(done, axis=0)


def invert_factors(gram):
    width = gram.shape[1]
    eye_row = lax.broadcasted_iota(jnp.int32, (HALF, HALF), 0)
    eye = (eye_row == lax.broadcasted_iota(jnp.int32, (HALF, HALF), 1)).astype(jnp.float32)
    lanes = lax.broadcasted_iota(jnp.int32, (HALF, width), 1)
    for low in range(0, width, HALF):
        high = low + HALF
        block = jnp.concatenate([gram[m, low:high, low:high] for m in range(2)], axis=1)
        both = inverse_factor_pair([block[8 * r : 8 * r + 8] for r in range(8)])
        for m in range(2):
            gram[m, low:high, low:high] = eye
            panel = product(both[:, HALF * m : HALF * m + HALF], gram[m, low:high, :], 1, 0)
            if high < width:
                gram[m, high:, low:high] = jnp.zeros((width - high, HALF), jnp.float32)
                gram[m, high:, :] = gram[m, high:, :] - product(panel[:, high:], panel, 0, 0)
                panel = jnp.where(lanes < high, panel, 0.0)
            gram[m, low:high, :] = panel


def rotate_kernel(top_ref, low_ref, new_top_ref, new_low_ref, gram, cross, norm, turn):
    rows, width = top_ref.shape
    cross[...] = jnp.zeros_like(cross)
    norm[...] = jnp.zeros_like(norm)

    @pl.loop(0, rows // CHUNK)
    def _(i):
        part = pl.ds(pl.multiple_of(i * CHUNK, CHUNK), CHUNK)
        top, low = top_ref[part, :], low_ref[part, :]
        cross[...] += lax.dot_general(
            top, low, (((0,), (0,)), ((), ())), preferred_element_type=jnp.float32
        )
        for m, block in enumerate((top, low)):
            wide = block.astype(jnp.float32)
            norm[m] += jnp.sum((wide * wide).reshape(CHUNK // 8, 8, width), axis=0)

    norm_top = jnp.broadcast_to(jnp.sum(norm[0], axis=0, keepdims=True), (width, width)).T
    norm_low = jnp.sum(norm[1], axis=0, keepdims=True)
    coupling = 2.0 * cross[...] / (norm_top + norm_low + epsilon)
    cross[...] = coupling
    row = lax.broadcasted_iota(jnp.int32, (width, width), 0)
    eye = (row == lax.broadcasted_iota(jnp.int32, (width, width), 1)).astype(jnp.float32)
    gram[0] = eye + product(coupling, coupling, 1, 1)
    gram[1] = eye + product(coupling, coupling, 0, 0)
    invert_factors(gram)
    turn[0:width, 0:width] = gram[0].T.astype(jnp.bfloat16)
    turn[0:width, width:] = product(cross[...], gram[1], 1, 1).astype(jnp.bfloat16)
    turn[width:, 0:width] = (-product(cross[...], gram[0], 0, 1)).astype(jnp.bfloat16)
    turn[width:, width:] = gram[1].T.astype(jnp.bfloat16)

    @pl.loop(0, rows // CHUNK)
    def _(i):
        part = pl.ds(pl.multiple_of(i * CHUNK, CHUNK), CHUNK)
        joined = jnp.concatenate([top_ref[part, :], low_ref[part, :]], axis=1)
        result = jnp.dot(joined, turn[...], preferred_element_type=jnp.float32).astype(jnp.bfloat16)
        new_top_ref[part, :] = result[:, :width]
        new_low_ref[part, :] = result[:, width:]


def rotate(top, low):
    width = top.shape[1]
    vmem = pl.BlockSpec(memory_space=pltpu.VMEM)
    return pl.pallas_call(
        rotate_kernel,
        out_shape=[jax.ShapeDtypeStruct(top.shape, top.dtype)] * 2,
        in_specs=[vmem, vmem],
        out_specs=[vmem, vmem],
        scratch_shapes=[
            pltpu.VMEM((2, width, width), jnp.float32),
            pltpu.VMEM((width, width), jnp.float32),
            pltpu.VMEM((2, 8, width), jnp.float32),
            pltpu.VMEM((2 * width, 2 * width), jnp.bfloat16),
        ],
        compiler_params=pltpu.CompilerParams(vmem_limit_bytes=32 * 2**20),
    )(top, low)


def ring_place(y, core):
    y = lax.rem(y + 4, 4)
    column = lax.axis_index("pair") // 2
    return {"group": (y // 2) * 2 + core, "pair": column * 2 + lax.rem(y, 2)}


def own_ring_position():
    group, pair = lax.axis_index("group"), lax.axis_index("pair")
    return (group // 2) * 2 + lax.rem(pair, 2), lax.rem(group, 2)


def regroup_kernel(choice, slots, top_ref, low_ref, landed, passed, send, recv, pass_send):
    y, core = own_ring_position()
    side = lax.rem(y, 2)
    chunks = recv.shape[1]
    rows = slots.shape[1] // chunks

    barrier = pltpu.get_barrier_semaphore()
    for step in (1, -1):
        for other in range(2):
            pl.semaphore_signal(barrier, inc=1, device_id=ring_place(y + step, other))
    pl.semaphore_signal(barrier, inc=1, device_id=ring_place(y, 1 - core))
    pl.semaphore_wait(barrier, 5)

    def part(i):
        return pl.ds(i * rows, rows)

    def away(slot, i):
        step = 1 if slot == 1 else -1
        place = core if slot == 1 else 2 + core
        return pltpu.make_async_remote_copy(
            src_ref=slots.at[slot, part(i)],
            dst_ref=landed.at[place, part(i)],
            send_sem=send.at[slot, i],
            recv_sem=recv.at[place, i],
            device_id=ring_place(y + step, side),
        )

    def across(i):
        return pltpu.make_async_remote_copy(
            src_ref=slots.at[0, part(i)],
            dst_ref=landed.at[core, part(i)],
            send_sem=send.at[0, i],
            recv_sem=recv.at[core, i],
            device_id=ring_place(y, 1 - core),
        )

    def stay(i):
        return pltpu.make_async_copy(slots.at[0, part(i)], landed.at[core, part(i)], recv.at[core, i])

    def onward(way, i):
        return pltpu.make_async_remote_copy(
            src_ref=passed.at[way, part(i)],
            dst_ref=landed.at[2 + way, part(i)],
            send_sem=pass_send.at[way, i],
            recv_sem=recv.at[2 + way, i],
            device_id=ring_place(y + (1 if way == 0 else -1), core),
        )

    def arrival(place, i):
        here = landed.at[place, part(i)]
        pltpu.make_async_copy(here, here, recv.at[place, i]).wait()

    for i in range(chunks):
        for slot in (1, 2):
            away(slot, i).start()

    @pl.when(core == side)
    def _():
        for i in range(chunks):
            stay(i).start()

    @pl.when(core != side)
    def _():
        for i in range(chunks):
            across(i).start()

    for i in range(chunks):
        for place in range(4):
            arrival(place, i)
            if place % 2 == 1:
                way = place // 2

                @pl.when(core != side)
                def _():
                    first, second = landed[2 * way, part(i)], landed[2 * way + 1, part(i)]
                    passed[way, part(i)] = jnp.where(choice[way] > 0, second, first)
                    onward(way, i).start()

        for place, out in ((2, top_ref), (3, low_ref)):
            which = choice[place]
            lower = jnp.where(which == 0, landed[0, part(i)], landed[1, part(i)])
            upper = jnp.where(which == 2, landed[2, part(i)], landed[3, part(i)])
            out[part(i), :] = jnp.where(which < 2, lower, upper)

    for i in range(chunks):
        for slot in (1, 2):
            away(slot, i).wait_send()

        @pl.when(core != side)
        def _():
            across(i).wait_send()
            for way in range(2):
                onward(way, i).wait_send()


def regroup(slots, choice):
    _, rows, width = slots.shape
    vmem = pl.BlockSpec(memory_space=pltpu.VMEM)
    chunks = 4
    return pl.pallas_call(
        regroup_kernel,
        out_shape=[jax.ShapeDtypeStruct((rows, width), slots.dtype)] * 2,
        in_specs=[pl.BlockSpec(memory_space=pltpu.SMEM), pl.BlockSpec(memory_space=pl.ANY)],
        out_specs=[vmem, vmem],
        scratch_shapes=[
            pltpu.VMEM((4, rows, width), slots.dtype),
            pltpu.VMEM((2, rows, width), slots.dtype),
            pltpu.SemaphoreType.DMA((3, chunks)),
            pltpu.SemaphoreType.DMA((4, chunks)),
            pltpu.SemaphoreType.DMA((2, chunks)),
        ],
        compiler_params=pltpu.CompilerParams(
            collective_id=0, has_side_effects=True, vmem_limit_bytes=32 * 2**20
        ),
    )(choice, slots)


def slot_codes(dest_group):
    table = dest_group.reshape(4, 32, 2)
    chip = (jnp.arange(4)[:, None] // 2) * 2 + jnp.arange(32)[None, :] % 2
    distance = (table - chip[:, :, None] + 4) % 4
    other = distance[:, :, ::-1]
    slot = jnp.where(distance == 3, 2, distance)
    slot = jnp.where(distance == 2, jnp.where(other == 1, 2, 1), slot)
    return table, distance, slot


def choices(table, distance, slot):
    y, core = own_ring_position()
    column = lax.axis_index("pair") // 2
    pair = column * 2 + core
    dist, slots, dest = (
        lax.dynamic_index_in_dim(array, pair, 1, keepdims=False) for array in (distance, slot, table)
    )
    far = jnp.where(dist == 2, slots, 0)
    after, before = ((y + 3) % 4) // 2 * 2 + 1, ((y + 1) % 4) // 2 * 2 + 1
    second = jnp.arange(4)
    pass_up = jnp.sum(jnp.where((second == after)[:, None] & (far == 1), 1, 0))
    pass_down = jnp.sum(jnp.where((second == before)[:, None] & (far == 2), 1, 0))
    origin = second % 2
    place = jnp.where(
        dist % 2 == 1,
        origin[:, None] + jnp.where(dist == 1, 0, 2),
        jnp.where(dist == 0, origin[:, None], 1 + slots),
    )
    wanted = jnp.sum(jnp.where(dest == y, place, 0), axis=0)
    return jnp.stack([pass_up, pass_down, wanted[0], wanted[1]]).astype(jnp.int32)


def home(t, p):
    return t * 32 + p


def working_place(t, p):
    return ((t // 2) * 2 + p % 2) * 32 + (p // 2) * 2 + t % 2


def moved(array, source, target, by):
    pairs = [(source(t, p), target(t, (p + by) % 32)) for t in range(4) for p in range(32)]
    return lax.ppermute(array, ("group", "pair"), pairs)


def body(genotypes, dest_group):
    width = genotypes.shape[1] // 2
    scaled = standardize(genotypes)
    table, distance, slot = slot_codes(dest_group)
    own_slot = lax.dynamic_index_in_dim(slot, lax.axis_index("pair"), 1, keepdims=False)
    own_slot = lax.dynamic_index_in_dim(own_slot, lax.axis_index("group"), 0, keepdims=False)
    takes_first = (jnp.arange(3) == own_slot[0])[:, None, None]
    slots = jnp.where(takes_first, scaled[None, :, :width], scaled[None, :, width:])
    top, low = regroup(slots, choices(table, distance, slot))
    for cycle_round in range(ROUNDS):
        top, low = rotate(top, low)
        if cycle_round < ROUNDS - 1:
            low = moved(low, working_place, working_place, 1)
    top = moved(top, working_place, home, 0)
    low = moved(low, working_place, home, 1)
    return jnp.concatenate([top, low], axis=1)


def solution(mesh):
    in_specs = (P(None, ("group", "pair")), P())
    out_specs = P(None, ("group", "pair"))
    return jax.shard_map(body, mesh=mesh, in_specs=in_specs, out_specs=out_specs, check_vma=False)
```

```python
import jax
import jax.numpy as jnp
from jax import lax
from jax.experimental import pallas as pl
from jax.experimental.pallas import tpu as pltpu
from jax.sharding import PartitionSpec as P

ROUNDS = 3
HALF = 64
CHUNK = 512

epsilon = 1e-05


def standardize(counts):
    values = counts.astype(jnp.float32)
    col_mean = jnp.mean(values, axis=0)
    centred = values - col_mean
    col_var = jnp.mean(centred * centred, axis=0)
    return (centred / jnp.sqrt(col_var + epsilon)).astype(jnp.bfloat16)


def product(left, right, left_dim, right_dim):
    dims = (((left_dim,), (right_dim,)), ((), ()))
    return lax.dot_general(
        left, right, dims, precision=lax.Precision.HIGHEST, preferred_element_type=jnp.float32
    )


def spread(tile, row):
    return jnp.broadcast_to(tile[row : row + 1, :], tile.shape)


def inverse_factor_pair(rows):
    lane = lax.broadcasted_iota(jnp.int32, (8, 128), 1)
    sub = lax.broadcasted_iota(jnp.int32, (8, 128), 0)
    start = jnp.where(lane < HALF, 0, HALF)
    col = lane - start
    rows = list(rows)
    pivots = [jnp.ones((8, 128), jnp.float32)] * 8
    for first in range(0, HALF, 8):
        tile = first // 8
        cols = [
            [jnp.take_along_axis(rows[r], start + (first + m), axis=1) for r in range(tile, 8)]
            for m in range(8)
        ]
        for m in range(8):
            here = col == first + m
            pivot = spread(cols[m][0], m)
            inverse = 1.0 / pivot
            pivots[tile] = jnp.where(sub == m, pivot, pivots[tile])
            cols[m][0] = jnp.where(sub > m, cols[m][0], 0.0)
            for n in range(m + 1, 8):
                ratio = spread(cols[n][0], m) * inverse
                cols[n] = [c - f * ratio for c, f in zip(cols[n], cols[m])]
            scaled = jnp.where(here, 1.0, spread(rows[tile], m)) * inverse
            for r in range(tile, 8):
                rows[r] = jnp.where(here, 0.0, rows[r]) - cols[m][r - tile] * scaled
    done = []
    for r in range(8):
        row = sub + 8 * r
        scale = lax.rsqrt(pivots[r])
        done.append(jnp.where(col < row, rows[r] * scale, jnp.where(col == row, scale, 0.0)))
    return jnp.concatenate(done, axis=0)


def invert_factors(gram):
    width = gram.shape[1]
    eye_row = lax.broadcasted_iota(jnp.int32, (HALF, HALF), 0)
    eye = (eye_row == lax.broadcasted_iota(jnp.int32, (HALF, HALF), 1)).astype(jnp.float32)
    lanes = lax.broadcasted_iota(jnp.int32, (HALF, width), 1)
    for low in range(0, width, HALF):
        high = low + HALF
        block = jnp.concatenate([gram[m, low:high, low:high] for m in range(2)], axis=1)
        both = inverse_factor_pair([block[8 * r : 8 * r + 8] for r in range(8)])
        for m in range(2):
            gram[m, low:high, low:high] = eye
            panel = product(both[:, HALF * m : HALF * m + HALF], gram[m, low:high, :], 1, 0)
            if high < width:
                gram[m, high:, low:high] = jnp.zeros((width - high, HALF), jnp.float32)
                gram[m, high:, :] = gram[m, high:, :] - product(panel[:, high:], panel, 0, 0)
                panel = jnp.where(lanes < high, panel, 0.0)
            gram[m, low:high, :] = panel


def rotation_into(turn, gram, cross, norm):
    width = cross.shape[0]
    norm_top = jnp.broadcast_to(jnp.sum(norm[0], axis=0, keepdims=True), (width, width)).T
    norm_low = jnp.sum(norm[1], axis=0, keepdims=True)
    coupling = 2.0 * cross[...] / (norm_top + norm_low + epsilon)
    cross[...] = coupling
    row = lax.broadcasted_iota(jnp.int32, (width, width), 0)
    eye = (row == lax.broadcasted_iota(jnp.int32, (width, width), 1)).astype(jnp.float32)
    gram[0] = eye + product(coupling, coupling, 1, 1)
    gram[1] = eye + product(coupling, coupling, 0, 0)
    invert_factors(gram)
    turn[0:width, 0:width] = gram[0].T.astype(jnp.bfloat16)
    turn[0:width, width:] = product(cross[...], gram[1], 1, 1).astype(jnp.bfloat16)
    turn[width:, 0:width] = (-product(cross[...], gram[0], 0, 1)).astype(jnp.bfloat16)
    turn[width:, width:] = gram[1].T.astype(jnp.bfloat16)


def rounds_kernel(
    top_in, low_in, top_out, low_out,
    top, lows, staged, gram, cross, norm, turn, local, send, recv, top_send, top_recv, low_send, low_recv,
):
    rows, width = top.shape
    chunks = rows // CHUNK
    y, core = own_ring_position()
    y_low = lax.rem(y, 2)
    y_base = y - y_low
    column = lax.axis_index("pair") // 2
    ahead = lax.rem(column + core, 16)
    behind = lax.rem(column + core + 15, 16)

    def device(column, y, core):
        return {"group": (y // 2) * 2 + core, "pair": column * 2 + lax.rem(y, 2)}

    next_device = device(ahead, y, 1 - core)
    last_device = device(behind, y, 1 - core)
    top_device = device(column, y_base + core, y_low)
    low_device = device(ahead, y_base + 1 - core, y_low)
    low_source = device(lax.rem(column + y_low + 15, 16), y_base + core, 1 - y_low)

    barrier = pltpu.get_barrier_semaphore()
    for other in (next_device, last_device, low_device, low_source):
        pl.semaphore_signal(barrier, inc=1, device_id=other)

    @pl.when(core != y_low)
    def _():
        pl.semaphore_signal(barrier, inc=1, device_id=top_device)
        pl.semaphore_wait(barrier, 5)

    @pl.when(core == y_low)
    def _():
        pl.semaphore_wait(barrier, 4)

    def part(i):
        return pl.ds(pl.multiple_of(i * CHUNK, CHUNK), CHUNK)

    first_top = pltpu.make_async_copy(top_in, top, local.at[0])
    first_low = pltpu.make_async_copy(low_in, lows.at[0], local.at[1])
    first_top.start()
    first_low.start()
    first_top.wait()
    first_low.wait()

    def shift(r, i):
        return pltpu.make_async_remote_copy(
            src_ref=staged.at[r, part(i)],
            dst_ref=lows.at[r + 1, part(i)],
            send_sem=send.at[r, i],
            recv_sem=recv.at[r, i],
            device_id=next_device,
        )

    def top_home(i):
        return pltpu.make_async_remote_copy(
            src_ref=top.at[part(i)],
            dst_ref=top_out.at[part(i)],
            send_sem=top_send.at[i],
            recv_sem=top_recv.at[i],
            device_id=top_device,
        )

    def top_stays(i):
        return pltpu.make_async_copy(top.at[part(i)], top_out.at[part(i)], top_recv.at[i])

    def low_home(i):
        return pltpu.make_async_remote_copy(
            src_ref=staged.at[ROUNDS - 1, part(i)],
            dst_ref=low_out.at[part(i)],
            send_sem=low_send.at[i],
            recv_sem=low_recv.at[i],
            device_id=low_device,
        )

    @pl.loop(0, ROUNDS)
    def _(r):
        cross[...] = jnp.zeros_like(cross)
        norm[...] = jnp.zeros_like(norm)

        @pl.loop(0, chunks)
        def _(i):
            @pl.when(r > 0)
            def _():
                shift(r - 1, i).wait_recv()

            blocks = top[part(i), :], lows[r, part(i), :]
            cross[...] += lax.dot_general(
                *blocks, (((0,), (0,)), ((), ())), preferred_element_type=jnp.float32
            )
            for m, block in enumerate(blocks):
                wide = block.astype(jnp.float32)
                norm[m] += jnp.sum((wide * wide).reshape(CHUNK // 8, 8, width), axis=0)

        rotation_into(turn, gram, cross, norm)

        @pl.loop(0, chunks)
        def _(i):
            joined = jnp.concatenate([top[part(i), :], lows[r, part(i), :]], axis=1)
            result = jnp.dot(joined, turn[...], preferred_element_type=jnp.float32)
            result = result.astype(jnp.bfloat16)
            staged[r, part(i), :] = result[:, width:]
            top[part(i), :] = result[:, :width]

            @pl.when(r < ROUNDS - 1)
            def _():
                shift(r, i).start()

            @pl.when(r == ROUNDS - 1)
            def _():
                low_home(i).start()

                @pl.when(core != y_low)
                def _():
                    top_home(i).start()

                @pl.when(core == y_low)
                def _():
                    top_stays(i).start()

    @pl.loop(0, chunks)
    def _(i):
        for r in range(ROUNDS - 1):
            shift(r, i).wait_send()
        low_home(i).wait()

        @pl.when(core != y_low)
        def _():
            top_home(i).wait()

        @pl.when(core == y_low)
        def _():
            top_stays(i).wait()


def play_rounds(top, low):
    rows, width = top.shape
    chunks = rows // CHUNK
    anywhere = pl.BlockSpec(memory_space=pl.ANY)
    dma = pltpu.SemaphoreType.DMA
    return pl.pallas_call(
        rounds_kernel,
        out_shape=[jax.ShapeDtypeStruct(top.shape, top.dtype)] * 2,
        in_specs=[anywhere, anywhere],
        out_specs=[anywhere, anywhere],
        scratch_shapes=[
            pltpu.VMEM((rows, width), top.dtype),
            pltpu.VMEM((ROUNDS, rows, width), top.dtype),
            pltpu.VMEM((ROUNDS, rows, width), top.dtype),
            pltpu.VMEM((2, width, width), jnp.float32),
            pltpu.VMEM((width, width), jnp.float32),
            pltpu.VMEM((2, 8, width), jnp.float32),
            pltpu.VMEM((2 * width, 2 * width), jnp.bfloat16),
            dma((2,)),
            dma((ROUNDS - 1, chunks)),
            dma((ROUNDS - 1, chunks)),
            dma((chunks,)),
            dma((chunks,)),
            dma((chunks,)),
            dma((chunks,)),
        ],
        compiler_params=pltpu.CompilerParams(
            collective_id=1, has_side_effects=True, vmem_limit_bytes=40 * 2**20
        ),
    )(top, low)


def ring_place(y, core):
    y = lax.rem(y + 4, 4)
    column = lax.axis_index("pair") // 2
    return {"group": (y // 2) * 2 + core, "pair": column * 2 + lax.rem(y, 2)}


def own_ring_position():
    group, pair = lax.axis_index("group"), lax.axis_index("pair")
    return (group // 2) * 2 + lax.rem(pair, 2), lax.rem(group, 2)


def regroup_kernel(choice, slots, top_ref, low_ref, landed, passed, send, recv, pass_send):
    y, core = own_ring_position()
    side = lax.rem(y, 2)
    chunks = recv.shape[1]
    rows = slots.shape[1] // chunks

    barrier = pltpu.get_barrier_semaphore()
    for step in (1, -1):
        for other in range(2):
            pl.semaphore_signal(barrier, inc=1, device_id=ring_place(y + step, other))
    pl.semaphore_signal(barrier, inc=1, device_id=ring_place(y, 1 - core))
    pl.semaphore_wait(barrier, 5)

    def part(i):
        return pl.ds(i * rows, rows)

    def away(slot, i):
        step = 1 if slot == 1 else -1
        place = core if slot == 1 else 2 + core
        return pltpu.make_async_remote_copy(
            src_ref=slots.at[slot, part(i)],
            dst_ref=landed.at[place, part(i)],
            send_sem=send.at[slot, i],
            recv_sem=recv.at[place, i],
            device_id=ring_place(y + step, side),
        )

    def across(i):
        return pltpu.make_async_remote_copy(
            src_ref=slots.at[0, part(i)],
            dst_ref=landed.at[core, part(i)],
            send_sem=send.at[0, i],
            recv_sem=recv.at[core, i],
            device_id=ring_place(y, 1 - core),
        )

    def stay(i):
        return pltpu.make_async_copy(slots.at[0, part(i)], landed.at[core, part(i)], recv.at[core, i])

    def onward(way, i):
        return pltpu.make_async_remote_copy(
            src_ref=passed.at[way, part(i)],
            dst_ref=landed.at[2 + way, part(i)],
            send_sem=pass_send.at[way, i],
            recv_sem=recv.at[2 + way, i],
            device_id=ring_place(y + (1 if way == 0 else -1), core),
        )

    def arrival(place, i):
        here = landed.at[place, part(i)]
        pltpu.make_async_copy(here, here, recv.at[place, i]).wait()

    for i in range(chunks):
        for slot in (1, 2):
            away(slot, i).start()

    @pl.when(core == side)
    def _():
        for i in range(chunks):
            stay(i).start()

    @pl.when(core != side)
    def _():
        for i in range(chunks):
            across(i).start()

    for i in range(chunks):
        for place in range(4):
            arrival(place, i)
            if place % 2 == 1:
                way = place // 2

                @pl.when(core != side)
                def _():
                    first, second = landed[2 * way, part(i)], landed[2 * way + 1, part(i)]
                    passed[way, part(i)] = jnp.where(choice[way] > 0, second, first)
                    onward(way, i).start()

        for place, out in ((2, top_ref), (3, low_ref)):
            which = choice[place]
            lower = jnp.where(which == 0, landed[0, part(i)], landed[1, part(i)])
            upper = jnp.where(which == 2, landed[2, part(i)], landed[3, part(i)])
            out[part(i), :] = jnp.where(which < 2, lower, upper)

    for i in range(chunks):
        for slot in (1, 2):
            away(slot, i).wait_send()

        @pl.when(core != side)
        def _():
            across(i).wait_send()
            for way in range(2):
                onward(way, i).wait_send()


def regroup(slots, choice):
    _, rows, width = slots.shape
    vmem = pl.BlockSpec(memory_space=pltpu.VMEM)
    chunks = 4
    return pl.pallas_call(
        regroup_kernel,
        out_shape=[jax.ShapeDtypeStruct((rows, width), slots.dtype)] * 2,
        in_specs=[pl.BlockSpec(memory_space=pltpu.SMEM), pl.BlockSpec(memory_space=pl.ANY)],
        out_specs=[vmem, vmem],
        scratch_shapes=[
            pltpu.VMEM((4, rows, width), slots.dtype),
            pltpu.VMEM((2, rows, width), slots.dtype),
            pltpu.SemaphoreType.DMA((3, chunks)),
            pltpu.SemaphoreType.DMA((4, chunks)),
            pltpu.SemaphoreType.DMA((2, chunks)),
        ],
        compiler_params=pltpu.CompilerParams(
            collective_id=0, has_side_effects=True, vmem_limit_bytes=32 * 2**20
        ),
    )(choice, slots)


def slot_codes(dest_group):
    table = dest_group.reshape(4, 32, 2)
    chip = (jnp.arange(4)[:, None] // 2) * 2 + jnp.arange(32)[None, :] % 2
    distance = (table - chip[:, :, None] + 4) % 4
    other = distance[:, :, ::-1]
    slot = jnp.where(distance == 3, 2, distance)
    slot = jnp.where(distance == 2, jnp.where(other == 1, 2, 1), slot)
    return table, distance, slot


def choices(table, distance, slot):
    y, core = own_ring_position()
    column = lax.axis_index("pair") // 2
    pair = column * 2 + core
    dist, slots, dest = (
        lax.dynamic_index_in_dim(array, pair, 1, keepdims=False) for array in (distance, slot, table)
    )
    far = jnp.where(dist == 2, slots, 0)
    after, before = ((y + 3) % 4) // 2 * 2 + 1, ((y + 1) % 4) // 2 * 2 + 1
    second = jnp.arange(4)
    pass_up = jnp.sum(jnp.where((second == after)[:, None] & (far == 1), 1, 0))
    pass_down = jnp.sum(jnp.where((second == before)[:, None] & (far == 2), 1, 0))
    origin = second % 2
    place = jnp.where(
        dist % 2 == 1,
        origin[:, None] + jnp.where(dist == 1, 0, 2),
        jnp.where(dist == 0, origin[:, None], 1 + slots),
    )
    wanted = jnp.sum(jnp.where(dest == y, place, 0), axis=0)
    return jnp.stack([pass_up, pass_down, wanted[0], wanted[1]]).astype(jnp.int32)


def body(genotypes, dest_group):
    width = genotypes.shape[1] // 2
    scaled = standardize(genotypes)
    table, distance, slot = slot_codes(dest_group)
    own_slot = lax.dynamic_index_in_dim(slot, lax.axis_index("pair"), 1, keepdims=False)
    own_slot = lax.dynamic_index_in_dim(own_slot, lax.axis_index("group"), 0, keepdims=False)
    takes_first = (jnp.arange(3) == own_slot[0])[:, None, None]
    slots = jnp.where(takes_first, scaled[None, :, :width], scaled[None, :, width:])
    top, low = regroup(slots, choices(table, distance, slot))
    top, low = play_rounds(top, low)
    return jnp.concatenate([top, low], axis=1)


def solution(mesh):
    in_specs = (P(None, ("group", "pair")), P())
    out_specs = P(None, ("group", "pair"))
    return jax.shard_map(body, mesh=mesh, in_specs=in_specs, out_specs=out_specs, check_vma=False)
```

```python
import jax
import jax.numpy as jnp
from jax import lax
from jax.experimental import pallas as pl
from jax.experimental.pallas import tpu as pltpu
from jax.sharding import PartitionSpec as P

ROUNDS = 3
HALF = 64
CHUNK = 512
AHEAD = 4

epsilon = 1e-05


def product(left, right, left_dim, right_dim):
    dims = (((left_dim,), (right_dim,)), ((), ()))
    return lax.dot_general(
        left, right, dims, precision=lax.Precision.HIGHEST, preferred_element_type=jnp.float32
    )


def spread(tile, row):
    return jnp.broadcast_to(tile[row : row + 1, :], tile.shape)


def inverse_factor_pair(rows):
    lane = lax.broadcasted_iota(jnp.int32, (8, 128), 1)
    sub = lax.broadcasted_iota(jnp.int32, (8, 128), 0)
    start = jnp.where(lane < HALF, 0, HALF)
    col = lane - start
    rows = list(rows)
    pivots = [jnp.ones((8, 128), jnp.float32)] * 8
    for first in range(0, HALF, 8):
        tile = first // 8
        cols = [
            [jnp.take_along_axis(rows[r], start + (first + m), axis=1) for r in range(tile, 8)]
            for m in range(8)
        ]
        for m in range(8):
            here = col == first + m
            pivot = spread(cols[m][0], m)
            inverse = 1.0 / pivot
            pivots[tile] = jnp.where(sub == m, pivot, pivots[tile])
            cols[m][0] = jnp.where(sub > m, cols[m][0], 0.0)
            for n in range(m + 1, 8):
                ratio = spread(cols[n][0], m) * inverse
                cols[n] = [c - f * ratio for c, f in zip(cols[n], cols[m])]
            scaled = jnp.where(here, 1.0, spread(rows[tile], m)) * inverse
            for r in range(tile, 8):
                rows[r] = jnp.where(here, 0.0, rows[r]) - cols[m][r - tile] * scaled
    done = []
    for r in range(8):
        row = sub + 8 * r
        scale = lax.rsqrt(pivots[r])
        done.append(jnp.where(col < row, rows[r] * scale, jnp.where(col == row, scale, 0.0)))
    return jnp.concatenate(done, axis=0)


def diagonal_pair(packed):
    lane = lax.broadcasted_iota(jnp.int32, packed.shape, 1)
    first = lax.rem(lane, 2 * HALF) < HALF
    return jnp.concatenate([jnp.where(first, packed, 0.0), jnp.where(first, 0.0, packed)], axis=0)


def invert_factors(matrices):
    width = matrices[0].shape[0]
    count = width // HALF
    parts = range(0, width, HALF)
    grid = [
        [jnp.concatenate([m[i : i + HALF, j : j + HALF] for m in matrices], axis=1) for j in parts] for i in parts
    ]
    lane = lax.broadcasted_iota(jnp.int32, (HALF, 2 * HALF), 1)
    eye = (lax.broadcasted_iota(jnp.int32, lane.shape, 0) == lax.rem(lane, HALF)).astype(jnp.float32)
    none = jnp.zeros(lane.shape, jnp.float32)
    done = []
    for k in range(count):
        both = inverse_factor_pair([grid[k][k][8 * r : 8 * r + 8] for r in range(8)])
        row = jnp.concatenate([eye if j == k else grid[k][j] for j in range(count)], axis=1)
        panel = product(both, diagonal_pair(row), 1, 0)
        if k + 1 < count:
            corner, spread_panel = diagonal_pair(both), diagonal_pair(panel)
            for i in range(k + 1, count):
                below = product(product(grid[i][k], corner, 1, 1), spread_panel, 1, 0)
                grid[i][k] = none
                grid[i] = [grid[i][j] - below[:, 2 * HALF * j : 2 * HALF * (j + 1)] for j in range(count)]
        done.append([panel[:, 2 * HALF * j : 2 * HALF * (j + 1)] if j <= k else none for j in range(count)])
    return [
        jnp.concatenate(
            [jnp.concatenate([b[:, HALF * m : HALF * (m + 1)] for b in blocks], axis=1) for blocks in done], axis=0
        )
        for m in range(2)
    ]


def rotation_into(turns, r, cross, norm, right_is_there):
    width = cross.shape[0]
    norm_top = jnp.broadcast_to(jnp.sum(norm[0], axis=0, keepdims=True), (width, width)).T
    norm_low = jnp.sum(norm[1], axis=0, keepdims=True)
    coupling = 2.0 * cross[...] / (norm_top + norm_low + epsilon)
    cross[...] = coupling
    row = lax.broadcasted_iota(jnp.int32, (width, width), 0)
    eye = (row == lax.broadcasted_iota(jnp.int32, (width, width), 1)).astype(jnp.float32)
    top_inverse, low_inverse = invert_factors(
        [eye + product(coupling, coupling, 1, 1), eye + product(coupling, coupling, 0, 0)]
    )
    turns[r, 1, 0:width, :] = product(cross[...], low_inverse, 1, 1).astype(jnp.bfloat16)
    turns[r, 1, width:, :] = low_inverse.T.astype(jnp.bfloat16)
    right_is_there()
    turns[r, 0, 0:width, :] = top_inverse.T.astype(jnp.bfloat16)
    turns[r, 0, width:, :] = (-product(cross[...], top_inverse, 0, 1)).astype(jnp.bfloat16)


def own_ring_position():
    group, pair = lax.axis_index("group"), lax.axis_index("pair")
    return (group // 2) * 2 + lax.rem(pair, 2), lax.rem(group, 2)


def whole_kernel(
    choice, counts, top_out, low_out,
    read, slots, landed, passed, tops, lows, staged, shadow, shadow_low, cross, norm, turns, shadow_turns,
    read_sem, send, recv, pass_send, copy_send, copy_recv, move_send, move_recv, after_send, after_recv,
    turn_send, turn_recv, top_send, top_recv, low_send, low_recv,
):
    rows, width = tops.shape[1:]
    chunks = rows // CHUNK
    y, core = own_ring_position()
    side = lax.rem(y, 2)
    column = lax.axis_index("pair") // 2
    even = core == 0

    def device(ahead, y, core):
        y = lax.rem(y + 4, 4)
        there = lax.rem(column + ahead + 16, 16)
        return {"group": (y // 2) * 2 + core, "pair": there * 2 + lax.rem(y, 2)}

    def part(i):
        return pl.ds(pl.multiple_of(i * CHUNK, CHUNK), CHUNK)

    def reading(i):
        return pltpu.make_async_copy(counts.at[part(i)], read.at[part(i)], read_sem.at[i])

    @pl.loop(0, chunks)
    def _(i):
        reading(i).start()

    partner = device(0, y, 1 - core)
    after = device(1, y, 0)
    base = y - side
    top_device = device(0, base + core, side)
    low_device = device(core, base + 1 - core, side)
    low_source = device(side - 1, base + core, 1 - side)

    barrier = pltpu.get_barrier_semaphore()
    others = [partner, low_device, low_source]
    others += [device(0, y + step, c) for step in (1, -1) for c in (0, 1)]
    others += [device(step, y, c) for step in (1, -1) for c in (0, 1)]
    for other in others:
        pl.semaphore_signal(barrier, inc=1, device_id=other)

    @pl.when(core != side)
    def _():
        pl.semaphore_signal(barrier, inc=1, device_id=top_device)
        pl.semaphore_wait(barrier, len(others) + 1)

    @pl.when(core == side)
    def _():
        pl.semaphore_wait(barrier, len(others))


    def away(slot, i):
        place = core if slot == 1 else 2 + core
        return pltpu.make_async_remote_copy(
            src_ref=slots.at[slot, part(i)],
            dst_ref=landed.at[place, part(i)],
            send_sem=send.at[slot, i],
            recv_sem=recv.at[place, i],
            device_id=device(0, y + (1 if slot == 1 else -1), side),
        )

    def across(i):
        return pltpu.make_async_remote_copy(
            src_ref=slots.at[0, part(i)],
            dst_ref=landed.at[core, part(i)],
            send_sem=send.at[0, i],
            recv_sem=recv.at[core, i],
            device_id=partner,
        )

    def stay(i):
        return pltpu.make_async_copy(slots.at[0, part(i)], landed.at[core, part(i)], recv.at[core, i])

    def onward(way, i):
        return pltpu.make_async_remote_copy(
            src_ref=passed.at[way, part(i)],
            dst_ref=landed.at[2 + way, part(i)],
            send_sem=pass_send.at[way, i],
            recv_sem=recv.at[2 + way, i],
            device_id=device(0, y + (1 if way == 0 else -1), core),
        )

    def arrival(place, i):
        here = landed.at[place, part(i)]
        pltpu.make_async_copy(here, here, recv.at[place, i]).wait()


    def copied(m, i):
        source = tops if m == 0 else lows
        return pltpu.make_async_remote_copy(
            src_ref=source.at[0, part(i)],
            dst_ref=shadow.at[m, part(i)],
            send_sem=copy_send.at[m, i],
            recv_sem=copy_recv.at[m, i],
            device_id=after,
        )

    def turned(k):
        r, half = ((0, 1), (0, 0), (1, 1))[k]
        return pltpu.make_async_remote_copy(
            src_ref=turns.at[r, half],
            dst_ref=shadow_turns.at[k],
            send_sem=turn_send.at[k],
            recv_sem=turn_recv.at[k],
            device_id=after,
        )

    def followed(i):
        return pltpu.make_async_remote_copy(
            src_ref=staged.at[0, part(i)],
            dst_ref=shadow_low.at[part(i)],
            send_sem=after_send.at[i],
            recv_sem=after_recv.at[i],
            device_id=after,
        )

    def move(r, i):
        return pltpu.make_async_remote_copy(
            src_ref=staged.at[r, part(i)],
            dst_ref=lows.at[r + 1, part(i)],
            send_sem=move_send.at[r, i],
            recv_sem=move_recv.at[r, i],
            device_id=partner,
        )

    def top_home(i):
        return pltpu.make_async_remote_copy(
            src_ref=tops.at[1, part(i)],
            dst_ref=top_out.at[part(i)],
            send_sem=top_send.at[i],
            recv_sem=top_recv.at[i],
            device_id=top_device,
        )

    def top_stays(i):
        return pltpu.make_async_copy(tops.at[1, part(i)], top_out.at[part(i)], top_recv.at[i])

    def low_home(i):
        return pltpu.make_async_remote_copy(
            src_ref=staged.at[ROUNDS - 1, part(i)],
            dst_ref=low_out.at[part(i)],
            send_sem=low_send.at[i],
            recv_sem=low_recv.at[i],
            device_id=low_device,
        )


    def gather_sums(i, sums):
        reading(i).wait()
        values = read[part(i), :].astype(jnp.float32).reshape(CHUNK // 8, 8, 2 * width)
        return sums[0] + jnp.sum(values, axis=0), sums[1] + jnp.sum(values * values, axis=0)

    nothing = jnp.zeros((8, 2 * width), jnp.float32)
    sums = lax.fori_loop(0, chunks, gather_sums, (nothing, nothing))
    total, squares = (jnp.sum(one, axis=0, keepdims=True) for one in sums)
    mean = total * (1.0 / rows)
    whole = total.astype(jnp.int32)
    spread_of = (rows * squares.astype(jnp.int32) - whole * whole).astype(jnp.float32)
    factor = 1.0 / jnp.sqrt(spread_of * (1.0 / (rows * rows)) + epsilon)

    @pl.loop(0, chunks)
    def _(i):
        scaled = ((read[part(i), :].astype(jnp.float32) - mean) * factor).astype(jnp.bfloat16)
        for slot in range(3):
            slots[slot, part(i), :] = jnp.where(choice[4 + slot] > 0, scaled[:, :width], scaled[:, width:])

        @pl.when(i < AHEAD)
        def _():
            away(1, i).start()
            away(2, i).start()

        @pl.when(core == side)
        def _():
            stay(i).start()

        @pl.when(core != side)
        def _():
            across(i).start()

    def add_products(blocks):
        cross[...] += lax.dot_general(
            *blocks, (((0,), (0,)), ((), ())), preferred_element_type=jnp.float32
        )
        for m, block in enumerate(blocks):
            wide = block.astype(jnp.float32)
            norm[m] += jnp.sum((wide * wide).reshape(CHUNK // 8, 8, width), axis=0)

    def clear_products():
        cross[...] = jnp.zeros_like(cross)
        norm[...] = jnp.zeros_like(norm)

    clear_products()

    @pl.loop(0, chunks)
    def _(i):
        for way in range(2):
            for place in (2 * way, 2 * way + 1):
                arrival(place, i)

            @pl.when(core != side)
            def _():
                first, second = landed[2 * way, part(i)], landed[2 * way + 1, part(i)]
                passed[way, part(i)] = jnp.where(choice[way] > 0, second, first)
                onward(way, i).start()

        @pl.when(i < chunks - AHEAD)
        def _():
            away(1, i + AHEAD).start()
            away(2, i + AHEAD).start()

        blocks = []
        for place, target in ((2, tops), (3, lows)):
            which = choice[place]
            lower = jnp.where(which == 0, landed[0, part(i)], landed[1, part(i)])
            upper = jnp.where(which == 2, landed[2, part(i)], landed[3, part(i)])
            block = jnp.where(which < 2, lower, upper)
            target[0, part(i), :] = block
            blocks.append(block)

        @pl.when(jnp.logical_not(even))
        def _():
            copied(0, i).start()
            copied(1, i).start()

        add_products(blocks)

    def matmul(left, right, turn):
        joined = jnp.concatenate([left, right], axis=1)
        return jnp.dot(joined, turn, preferred_element_type=jnp.float32).astype(jnp.bfloat16)

    @pl.loop(0, ROUNDS)
    def _(r):
        here = jnp.minimum(r, 1)

        @pl.when(r > 0)
        def _():
            clear_products()

            @pl.when(even & (r == 1))
            def _():
                turned(0).wait_recv()

            @pl.when(even & (r == 2))
            def _():
                turned(1).wait_recv()

                @pl.loop(0, chunks)
                def _(i):
                    shadow[0, part(i)] = matmul(shadow[0, part(i)], shadow[1, part(i)], shadow_turns[1])

                turned(2).wait_recv()

            @pl.loop(0, chunks)
            def _(i):
                @pl.when(jnp.logical_not(even))
                def _():
                    move(r - 1, i).wait_recv()

                @pl.when(even & (r == 1))
                def _():
                    copied(0, i).wait_recv()
                    copied(1, i).wait_recv()
                    lows[1, part(i), :] = matmul(shadow[0, part(i)], shadow[1, part(i)], shadow_turns[0])

                @pl.when(even & (r == 2))
                def _():
                    followed(i).wait_recv()
                    lows[2, part(i), :] = matmul(shadow[0, part(i)], shadow_low[part(i)], shadow_turns[2])

                add_products([tops[1, part(i), :], lows[r, part(i), :]])

        def send_right():
            @pl.when(jnp.logical_not(even) & (r == 0))
            def _():
                turned(0).start()

            @pl.when(jnp.logical_not(even) & (r == 1))
            def _():
                turned(2).start()

        rotation_into(turns, r, cross, norm, send_right)

        @pl.when(jnp.logical_not(even) & (r == 0))
        def _():
            turned(1).start()

        @pl.loop(0, chunks)
        def _(i):
            top, low = tops[here, part(i), :], lows[r, part(i), :]

            @pl.when(even | (r == ROUNDS - 1))
            def _():
                staged[r, part(i), :] = matmul(top, low, turns[r, 1])

            @pl.when(even & (r < ROUNDS - 1))
            def _():
                move(r, i).start()

            @pl.when(even & (r == 0))
            def _():
                followed(i).start()

            @pl.when(r == ROUNDS - 1)
            def _():
                low_home(i).start()

            tops[1, part(i), :] = matmul(top, low, turns[r, 0])

            @pl.when((r == ROUNDS - 1) & (core != side))
            def _():
                top_home(i).start()

            @pl.when((r == ROUNDS - 1) & (core == side))
            def _():
                top_stays(i).start()

    @pl.when(jnp.logical_not(even))
    def _():
        for k in range(3):
            turned(k).wait_send()

    @pl.loop(0, chunks)
    def _(i):
        for slot in (1, 2):
            away(slot, i).wait_send()

        @pl.when(core != side)
        def _():
            across(i).wait_send()
            for way in range(2):
                onward(way, i).wait_send()
            top_home(i).wait()

        @pl.when(core == side)
        def _():
            top_stays(i).wait()

        @pl.when(even)
        def _():
            followed(i).wait_send()
            for r in range(ROUNDS - 1):
                move(r, i).wait_send()

        @pl.when(jnp.logical_not(even))
        def _():
            copied(0, i).wait_send()
            copied(1, i).wait_send()

        low_home(i).wait()


def play(choice, counts):
    rows, width = counts.shape[0], counts.shape[1] // 2
    chunks = rows // CHUNK
    anywhere = pl.BlockSpec(memory_space=pl.ANY)

    def blocks(count):
        return pltpu.VMEM((count, rows, width), jnp.bfloat16)

    def dma(*shape):
        return pltpu.SemaphoreType.DMA(shape)

    return pl.pallas_call(
        whole_kernel,
        out_shape=[jax.ShapeDtypeStruct((rows, width), jnp.bfloat16)] * 2,
        in_specs=[pl.BlockSpec(memory_space=pltpu.SMEM), anywhere],
        out_specs=[anywhere, anywhere],
        scratch_shapes=[
            pltpu.VMEM((rows, 2 * width), jnp.int32),
            blocks(3),
            blocks(4),
            blocks(2),
            blocks(2),
            blocks(ROUNDS),
            blocks(ROUNDS),
            blocks(2),
            pltpu.VMEM((rows, width), jnp.bfloat16),
            pltpu.VMEM((width, width), jnp.float32),
            pltpu.VMEM((2, 8, width), jnp.float32),
            pltpu.VMEM((ROUNDS, 2, 2 * width, width), jnp.bfloat16),
            pltpu.VMEM((3, 2 * width, width), jnp.bfloat16),
            dma(chunks),
            dma(3, chunks),
            dma(4, chunks),
            dma(2, chunks),
            dma(2, chunks),
            dma(2, chunks),
            dma(ROUNDS - 1, chunks),
            dma(ROUNDS - 1, chunks),
            dma(chunks),
            dma(chunks),
            dma(3),
            dma(3),
            dma(chunks),
            dma(chunks),
            dma(chunks),
            dma(chunks),
        ],
        compiler_params=pltpu.CompilerParams(
            collective_id=0, has_side_effects=True, vmem_limit_bytes=60 * 2**20
        ),
    )(choice, counts)


def slot_codes(dest_group):
    table = dest_group.reshape(4, 32, 2)
    chip = (jnp.arange(4)[:, None] // 2) * 2 + jnp.arange(32)[None, :] % 2
    distance = (table - chip[:, :, None] + 4) % 4
    other = distance[:, :, ::-1]
    slot = jnp.where(distance == 3, 2, distance)
    slot = jnp.where(distance == 2, jnp.where(other == 1, 2, 1), slot)
    return table, distance, slot


def choices(table, distance, slot):
    y, core = own_ring_position()
    column = lax.axis_index("pair") // 2
    pair = column * 2 + core
    dist, slots, dest = (
        lax.dynamic_index_in_dim(array, pair, 1, keepdims=False) for array in (distance, slot, table)
    )
    far = jnp.where(dist == 2, slots, 0)
    after, before = ((y + 3) % 4) // 2 * 2 + 1, ((y + 1) % 4) // 2 * 2 + 1
    second = jnp.arange(4)
    pass_up = jnp.sum(jnp.where((second == after)[:, None] & (far == 1), 1, 0))
    pass_down = jnp.sum(jnp.where((second == before)[:, None] & (far == 2), 1, 0))
    origin = second % 2
    place = jnp.where(
        dist % 2 == 1,
        origin[:, None] + jnp.where(dist == 1, 0, 2),
        jnp.where(dist == 0, origin[:, None], 1 + slots),
    )
    wanted = jnp.sum(jnp.where(dest == y, place, 0), axis=0)
    return jnp.stack([pass_up, pass_down, wanted[0], wanted[1]]).astype(jnp.int32)


def body(genotypes, dest_group):
    table, distance, slot = slot_codes(dest_group)
    own_slot = lax.dynamic_index_in_dim(slot, lax.axis_index("pair"), 1, keepdims=False)
    own_slot = lax.dynamic_index_in_dim(own_slot, lax.axis_index("group"), 0, keepdims=False)
    takes_first = (jnp.arange(3) == own_slot[0]).astype(jnp.int32)
    choice = jnp.concatenate([choices(table, distance, slot), takes_first])
    top, low = play(choice, genotypes)
    return jnp.concatenate([top, low], axis=1)


def solution(mesh):
    in_specs = (P(None, ("group", "pair")), P())
    out_specs = P(None, ("group", "pair"))
    return jax.shard_map(body, mesh=mesh, in_specs=in_specs, out_specs=out_specs, check_vma=False)
```

```python
import jax
import jax.numpy as jnp
from jax import lax
from jax.experimental import pallas as pl
from jax.experimental.pallas import tpu as pltpu
from jax.sharding import PartitionSpec as P

ROUNDS = 3
HALF = 64
CHUNK = 512
AHEAD = 2

epsilon = 1e-05


def product(left, right, left_dim, right_dim):
    dims = (((left_dim,), (right_dim,)), ((), ()))
    return lax.dot_general(
        left, right, dims, precision=lax.Precision.HIGHEST, preferred_element_type=jnp.float32
    )


def spread(tile, row):
    return jnp.broadcast_to(tile[row : row + 1, :], tile.shape)


def inverse_factor_pair(rows):
    lane = lax.broadcasted_iota(jnp.int32, (8, 128), 1)
    sub = lax.broadcasted_iota(jnp.int32, (8, 128), 0)
    start = jnp.where(lane < HALF, 0, HALF)
    col = lane - start
    rows = list(rows)
    pivots = [jnp.ones((8, 128), jnp.float32)] * 8
    for first in range(0, HALF, 8):
        tile = first // 8
        cols = [
            [jnp.take_along_axis(rows[r], start + (first + m), axis=1) for r in range(tile, 8)]
            for m in range(8)
        ]
        for m in range(8):
            here = col == first + m
            pivot = spread(cols[m][0], m)
            inverse = 1.0 / pivot
            pivots[tile] = jnp.where(sub == m, pivot, pivots[tile])
            cols[m][0] = jnp.where(sub > m, cols[m][0], 0.0)
            for n in range(m + 1, 8):
                ratio = spread(cols[n][0], m) * inverse
                cols[n] = [c - f * ratio for c, f in zip(cols[n], cols[m])]
            scaled = jnp.where(here, 1.0, spread(rows[tile], m)) * inverse
            for r in range(tile, 8):
                rows[r] = jnp.where(here, 0.0, rows[r]) - cols[m][r - tile] * scaled
    done = []
    for r in range(8):
        row = sub + 8 * r
        scale = lax.rsqrt(pivots[r])
        done.append(jnp.where(col < row, rows[r] * scale, jnp.where(col == row, scale, 0.0)))
    return jnp.concatenate(done, axis=0)


def diagonal_pair(packed):
    lane = lax.broadcasted_iota(jnp.int32, packed.shape, 1)
    first = lax.rem(lane, 2 * HALF) < HALF
    return jnp.concatenate([jnp.where(first, packed, 0.0), jnp.where(first, 0.0, packed)], axis=0)


def invert_factors(matrices):
    width = matrices[0].shape[0]
    count = width // HALF
    parts = range(0, width, HALF)
    grid = [
        [jnp.concatenate([m[i : i + HALF, j : j + HALF] for m in matrices], axis=1) for j in parts] for i in parts
    ]
    lane = lax.broadcasted_iota(jnp.int32, (HALF, 2 * HALF), 1)
    eye = (lax.broadcasted_iota(jnp.int32, lane.shape, 0) == lax.rem(lane, HALF)).astype(jnp.float32)
    none = jnp.zeros(lane.shape, jnp.float32)
    done = []
    for k in range(count):
        both = inverse_factor_pair([grid[k][k][8 * r : 8 * r + 8] for r in range(8)])
        row = jnp.concatenate([eye if j == k else grid[k][j] for j in range(count)], axis=1)
        panel = product(both, diagonal_pair(row), 1, 0)
        if k + 1 < count:
            corner, spread_panel = diagonal_pair(both), diagonal_pair(panel)
            for i in range(k + 1, count):
                below = product(product(grid[i][k], corner, 1, 1), spread_panel, 1, 0)
                grid[i][k] = none
                grid[i] = [grid[i][j] - below[:, 2 * HALF * j : 2 * HALF * (j + 1)] for j in range(count)]
        done.append([panel[:, 2 * HALF * j : 2 * HALF * (j + 1)] if j <= k else none for j in range(count)])
    return [
        jnp.concatenate(
            [jnp.concatenate([b[:, HALF * m : HALF * (m + 1)] for b in blocks], axis=1) for blocks in done], axis=0
        )
        for m in range(2)
    ]


def rotation_into(turns, r, cross, norm, right_is_there):
    width = cross.shape[0]
    norm_top = jnp.broadcast_to(jnp.sum(norm[0], axis=0, keepdims=True), (width, width)).T
    norm_low = jnp.sum(norm[1], axis=0, keepdims=True)
    coupling = 2.0 * cross[...] / (norm_top + norm_low + epsilon)
    cross[...] = coupling
    row = lax.broadcasted_iota(jnp.int32, (width, width), 0)
    eye = (row == lax.broadcasted_iota(jnp.int32, (width, width), 1)).astype(jnp.float32)
    top_inverse, low_inverse = invert_factors(
        [eye + product(coupling, coupling, 1, 1), eye + product(coupling, coupling, 0, 0)]
    )
    turns[r, 1, 0:width, :] = product(cross[...], low_inverse, 1, 1).astype(jnp.bfloat16)
    turns[r, 1, width:, :] = low_inverse.T.astype(jnp.bfloat16)
    right_is_there()
    turns[r, 0, 0:width, :] = top_inverse.T.astype(jnp.bfloat16)
    turns[r, 0, width:, :] = (-product(cross[...], top_inverse, 0, 1)).astype(jnp.bfloat16)


def own_ring_position():
    group, pair = lax.axis_index("group"), lax.axis_index("pair")
    return (group // 2) * 2 + lax.rem(pair, 2), lax.rem(group, 2)


def whole_kernel(
    dest, counts, top_out, low_out,
    read, slots, landed, passed, tops, lows, staged, shadow, shadow_low, cross, norm, turns, shadow_turns,
    read_sem, send, recv, pass_send, copy_send, copy_recv, move_send, move_recv, after_send, after_recv,
    turn_send, turn_recv, top_send, top_recv, low_send, low_recv,
):
    rows, width = tops.shape[1:]
    chunks = rows // CHUNK
    y, core = own_ring_position()
    side = lax.rem(y, 2)
    column = lax.axis_index("pair") // 2
    even = core == 0
    pass_second, wanted, first_slot = choices(dest)

    def device(ahead, y, core):
        y = lax.rem(y + 4, 4)
        there = lax.rem(column + ahead + 16, 16)
        return {"group": (y // 2) * 2 + core, "pair": there * 2 + lax.rem(y, 2)}

    def part(i):
        return pl.ds(pl.multiple_of(i * CHUNK, CHUNK), CHUNK)

    def reading(i):
        return pltpu.make_async_copy(counts.at[part(i)], read.at[part(i)], read_sem.at[i])

    @pl.loop(0, chunks)
    def _(i):
        reading(i).start()

    partner = device(0, y, 1 - core)
    after = device(1, y, 0)
    base = y - side
    top_device = device(0, base + core, side)
    low_device = device(core, base + 1 - core, side)
    low_source = device(side - 1, base + core, 1 - side)

    barrier = pltpu.get_barrier_semaphore()
    others = [partner, low_device, low_source]
    others += [device(0, y + step, c) for step in (1, -1) for c in (0, 1)]
    others += [device(step, y, c) for step in (1, -1) for c in (0, 1)]
    for other in others:
        pl.semaphore_signal(barrier, inc=1, device_id=other)

    @pl.when(core != side)
    def _():
        pl.semaphore_signal(barrier, inc=1, device_id=top_device)
        pl.semaphore_wait(barrier, len(others) + 1)

    @pl.when(core == side)
    def _():
        pl.semaphore_wait(barrier, len(others))


    def away(slot, i):
        place = core if slot == 1 else 2 + core
        return pltpu.make_async_remote_copy(
            src_ref=slots.at[slot, part(i)],
            dst_ref=landed.at[place, part(i)],
            send_sem=send.at[slot, i],
            recv_sem=recv.at[place, i],
            device_id=device(0, y + (1 if slot == 1 else -1), side),
        )

    def across(i):
        return pltpu.make_async_remote_copy(
            src_ref=slots.at[0, part(i)],
            dst_ref=landed.at[core, part(i)],
            send_sem=send.at[0, i],
            recv_sem=recv.at[core, i],
            device_id=partner,
        )

    def stay(i):
        return pltpu.make_async_copy(slots.at[0, part(i)], landed.at[core, part(i)], recv.at[core, i])

    def onward(way, i):
        return pltpu.make_async_remote_copy(
            src_ref=passed.at[way, part(i)],
            dst_ref=landed.at[2 + way, part(i)],
            send_sem=pass_send.at[way, i],
            recv_sem=recv.at[2 + way, i],
            device_id=device(0, y + (1 if way == 0 else -1), core),
        )

    def arrival(place, i):
        here = landed.at[place, part(i)]
        pltpu.make_async_copy(here, here, recv.at[place, i]).wait()


    def copied(m, i):
        source = tops if m == 0 else lows
        return pltpu.make_async_remote_copy(
            src_ref=source.at[0, part(i)],
            dst_ref=shadow.at[m, part(i)],
            send_sem=copy_send.at[m, i],
            recv_sem=copy_recv.at[m, i],
            device_id=after,
        )

    def turned(k):
        r, half = ((0, 1), (0, 0), (1, 1))[k]
        return pltpu.make_async_remote_copy(
            src_ref=turns.at[r, half],
            dst_ref=shadow_turns.at[k],
            send_sem=turn_send.at[k],
            recv_sem=turn_recv.at[k],
            device_id=after,
        )

    def followed(i):
        return pltpu.make_async_remote_copy(
            src_ref=staged.at[0, part(i)],
            dst_ref=shadow_low.at[part(i)],
            send_sem=after_send.at[i],
            recv_sem=after_recv.at[i],
            device_id=after,
        )

    def move(r, i):
        return pltpu.make_async_remote_copy(
            src_ref=staged.at[r, part(i)],
            dst_ref=lows.at[r + 1, part(i)],
            send_sem=move_send.at[r, i],
            recv_sem=move_recv.at[r, i],
            device_id=partner,
        )

    def top_home(i):
        return pltpu.make_async_remote_copy(
            src_ref=tops.at[1, part(i)],
            dst_ref=top_out.at[part(i)],
            send_sem=top_send.at[i],
            recv_sem=top_recv.at[i],
            device_id=top_device,
        )

    def top_stays(i):
        return pltpu.make_async_copy(tops.at[1, part(i)], top_out.at[part(i)], top_recv.at[i])

    def low_home(i):
        return pltpu.make_async_remote_copy(
            src_ref=staged.at[ROUNDS - 1, part(i)],
            dst_ref=low_out.at[part(i)],
            send_sem=low_send.at[i],
            recv_sem=low_recv.at[i],
            device_id=low_device,
        )


    def gather_sums(i, sums):
        reading(i).wait()
        values = read[part(i), :].astype(jnp.float32).reshape(CHUNK // 8, 8, 2 * width)
        return sums[0] + jnp.sum(values, axis=0), sums[1] + jnp.sum(values * values, axis=0)

    nothing = jnp.zeros((8, 2 * width), jnp.float32)
    sums = lax.fori_loop(0, chunks, gather_sums, (nothing, nothing))
    total, squares = (jnp.sum(one, axis=0, keepdims=True) for one in sums)
    mean = total * (1.0 / rows)
    whole = total.astype(jnp.int32)
    spread_of = (rows * squares.astype(jnp.int32) - whole * whole).astype(jnp.float32)
    factor = 1.0 / jnp.sqrt(spread_of * (1.0 / (rows * rows)) + epsilon)

    @pl.loop(0, chunks)
    def _(i):
        scaled = ((read[part(i), :].astype(jnp.float32) - mean) * factor).astype(jnp.bfloat16)
        for slot in range(3):
            slots[slot, part(i), :] = jnp.where(first_slot == slot, scaled[:, :width], scaled[:, width:])

        @pl.when(i < AHEAD)
        def _():
            away(1, i).start()
            away(2, i).start()

        @pl.when(core == side)
        def _():
            stay(i).start()

        @pl.when(core != side)
        def _():
            across(i).start()

    def add_products(blocks):
        cross[...] += lax.dot_general(
            *blocks, (((0,), (0,)), ((), ())), preferred_element_type=jnp.float32
        )
        for m, block in enumerate(blocks):
            wide = block.astype(jnp.float32)
            norm[m] += jnp.sum((wide * wide).reshape(CHUNK // 8, 8, width), axis=0)

    def clear_products():
        cross[...] = jnp.zeros_like(cross)
        norm[...] = jnp.zeros_like(norm)

    clear_products()

    @pl.loop(0, chunks)
    def _(i):
        for way in range(2):
            for place in (2 * way, 2 * way + 1):
                arrival(place, i)

            @pl.when(core != side)
            def _():
                first, second = landed[2 * way, part(i)], landed[2 * way + 1, part(i)]
                passed[way, part(i)] = jnp.where(pass_second[way] > 0, second, first)
                onward(way, i).start()

        @pl.when(i < chunks - AHEAD)
        def _():
            away(1, i + AHEAD).start()
            away(2, i + AHEAD).start()

        blocks = []
        for which, target in zip(wanted, (tops, lows)):
            lower = jnp.where(which == 0, landed[0, part(i)], landed[1, part(i)])
            upper = jnp.where(which == 2, landed[2, part(i)], landed[3, part(i)])
            block = jnp.where(which < 2, lower, upper)
            target[0, part(i), :] = block
            blocks.append(block)

        @pl.when(jnp.logical_not(even))
        def _():
            copied(0, i).start()
            copied(1, i).start()

        add_products(blocks)

    def matmul(left, right, turn):
        joined = jnp.concatenate([left, right], axis=1)
        return jnp.dot(joined, turn, preferred_element_type=jnp.float32).astype(jnp.bfloat16)

    @pl.loop(0, ROUNDS)
    def _(r):
        here = jnp.minimum(r, 1)

        @pl.when(r > 0)
        def _():
            clear_products()

            @pl.when(even & (r == 1))
            def _():
                turned(0).wait_recv()

            @pl.when(even & (r == 2))
            def _():
                turned(1).wait_recv()

                @pl.loop(0, chunks)
                def _(i):
                    shadow[0, part(i)] = matmul(shadow[0, part(i)], shadow[1, part(i)], shadow_turns[1])

                turned(2).wait_recv()

            @pl.loop(0, chunks)
            def _(i):
                @pl.when(jnp.logical_not(even))
                def _():
                    move(r - 1, i).wait_recv()

                @pl.when(even & (r == 1))
                def _():
                    copied(0, i).wait_recv()
                    copied(1, i).wait_recv()
                    lows[1, part(i), :] = matmul(shadow[0, part(i)], shadow[1, part(i)], shadow_turns[0])

                @pl.when(even & (r == 2))
                def _():
                    followed(i).wait_recv()
                    lows[2, part(i), :] = matmul(shadow[0, part(i)], shadow_low[part(i)], shadow_turns[2])

                add_products([tops[1, part(i), :], lows[r, part(i), :]])

        def send_right():
            @pl.when(jnp.logical_not(even) & (r == 0))
            def _():
                turned(0).start()

            @pl.when(jnp.logical_not(even) & (r == 1))
            def _():
                turned(2).start()

        rotation_into(turns, r, cross, norm, send_right)

        @pl.when(jnp.logical_not(even) & (r == 0))
        def _():
            turned(1).start()

        @pl.loop(0, chunks)
        def _(i):
            top, low = tops[here, part(i), :], lows[r, part(i), :]

            @pl.when(even | (r == ROUNDS - 1))
            def _():
                staged[r, part(i), :] = matmul(top, low, turns[r, 1])

            @pl.when(even & (r < ROUNDS - 1))
            def _():
                move(r, i).start()

            @pl.when(even & (r == 0))
            def _():
                followed(i).start()

            @pl.when(r == ROUNDS - 1)
            def _():
                low_home(i).start()

            tops[1, part(i), :] = matmul(top, low, turns[r, 0])

            @pl.when((r == ROUNDS - 1) & (core != side))
            def _():
                top_home(i).start()

            @pl.when((r == ROUNDS - 1) & (core == side))
            def _():
                top_stays(i).start()

    @pl.when(jnp.logical_not(even))
    def _():
        for k in range(3):
            turned(k).wait_send()

    @pl.loop(0, chunks)
    def _(i):
        for slot in (1, 2):
            away(slot, i).wait_send()

        @pl.when(core != side)
        def _():
            across(i).wait_send()
            for way in range(2):
                onward(way, i).wait_send()
            top_home(i).wait()

        @pl.when(core == side)
        def _():
            top_stays(i).wait()

        @pl.when(even)
        def _():
            followed(i).wait_send()
            for r in range(ROUNDS - 1):
                move(r, i).wait_send()

        @pl.when(jnp.logical_not(even))
        def _():
            copied(0, i).wait_send()
            copied(1, i).wait_send()

        low_home(i).wait()


def play(dest, counts):
    rows, width = counts.shape[0], counts.shape[1] // 2
    chunks = rows // CHUNK
    anywhere = pl.BlockSpec(memory_space=pl.ANY)

    def blocks(count):
        return pltpu.VMEM((count, rows, width), jnp.bfloat16)

    def dma(*shape):
        return pltpu.SemaphoreType.DMA(shape)

    return pl.pallas_call(
        whole_kernel,
        out_shape=[jax.ShapeDtypeStruct((rows, width), jnp.bfloat16)] * 2,
        in_specs=[pl.BlockSpec(memory_space=pltpu.SMEM), anywhere],
        out_specs=[anywhere, anywhere],
        scratch_shapes=[
            pltpu.VMEM((rows, 2 * width), jnp.int32),
            blocks(3),
            blocks(4),
            blocks(2),
            blocks(2),
            blocks(ROUNDS),
            blocks(ROUNDS),
            blocks(2),
            pltpu.VMEM((rows, width), jnp.bfloat16),
            pltpu.VMEM((width, width), jnp.float32),
            pltpu.VMEM((2, 8, width), jnp.float32),
            pltpu.VMEM((ROUNDS, 2, 2 * width, width), jnp.bfloat16),
            pltpu.VMEM((3, 2 * width, width), jnp.bfloat16),
            dma(chunks),
            dma(3, chunks),
            dma(4, chunks),
            dma(2, chunks),
            dma(2, chunks),
            dma(2, chunks),
            dma(ROUNDS - 1, chunks),
            dma(ROUNDS - 1, chunks),
            dma(chunks),
            dma(chunks),
            dma(3),
            dma(3),
            dma(chunks),
            dma(chunks),
            dma(chunks),
            dma(chunks),
        ],
        compiler_params=pltpu.CompilerParams(
            collective_id=0, has_side_effects=True, vmem_limit_bytes=55 * 2**20
        ),
    )(dest, counts)


def routed(dest, group, pair, side):
    chip = (group // 2) * 2 + lax.rem(pair, 2)
    distance, other = (lax.rem(dest[(group * 32 + pair) * 2 + k] - chip + 4, 4) for k in (side, 1 - side))
    slot = jnp.where(distance == 2, jnp.where(other == 1, 2, 1), jnp.where(distance == 3, 2, distance))
    return distance, slot


def choices(dest):
    y, core = own_ring_position()
    group, own_pair = lax.axis_index("group"), lax.axis_index("pair")
    pair = (own_pair // 2) * 2 + core

    def passing(chip, slot):
        distance, used = routed(dest, (chip // 2) * 2 + 1, pair, 0)
        other, other_used = routed(dest, (chip // 2) * 2 + 1, pair, 1)
        far = ((distance == 2) & (used == slot)) | ((other == 2) & (other_used == slot))
        return far.astype(jnp.int32)

    def landing(side):
        found = jnp.int32(0)
        for source in range(4):
            distance, slot = routed(dest, source, pair, side)
            origin = source % 2
            near = jnp.where(distance == 1, origin, 2 + origin)
            place = jnp.where(lax.rem(distance, 2) == 1, near, jnp.where(distance == 0, origin, 1 + slot))
            found = found + jnp.where(dest[(source * 32 + pair) * 2 + side] == y, place, 0)
        return found

    first = routed(dest, group, own_pair, 0)[1]
    return (
        (passing(lax.rem(y + 3, 4), 1), passing(lax.rem(y + 1, 4), 2)),
        (landing(0), landing(1)),
        first,
    )


def body(genotypes, dest_group):
    top, low = play(dest_group, genotypes)
    return jnp.concatenate([top, low], axis=1)


def solution(mesh):
    in_specs = (P(None, ("group", "pair")), P())
    out_specs = P(None, ("group", "pair"))
    return jax.shard_map(body, mesh=mesh, in_specs=in_specs, out_specs=out_specs, check_vma=False)
```

```python
import jax
import jax.numpy as jnp
from jax import lax
from jax.experimental import pallas as pl
from jax.experimental.pallas import tpu as pltpu
from jax.sharding import PartitionSpec as P

ROUNDS = 3
HALF = 64
CHUNK = 512
AHEAD = 2

epsilon = 1e-05


def product(left, right, left_dim, right_dim):
    dims = (((left_dim,), (right_dim,)), ((), ()))
    return lax.dot_general(
        left, right, dims, precision=lax.Precision.HIGHEST, preferred_element_type=jnp.float32
    )


def spread(tile, row):
    return jnp.broadcast_to(tile[row : row + 1, :], tile.shape)


def inverse_factor_pair(rows):
    lane = lax.broadcasted_iota(jnp.int32, (8, 128), 1)
    sub = lax.broadcasted_iota(jnp.int32, (8, 128), 0)
    start = jnp.where(lane < HALF, 0, HALF)
    col = lane - start
    rows = list(rows)
    pivots = [jnp.ones((8, 128), jnp.float32)] * 8
    for first in range(0, HALF, 8):
        tile = first // 8
        cols = [
            [jnp.take_along_axis(rows[r], start + (first + m), axis=1) for r in range(tile, 8)]
            for m in range(8)
        ]
        for m in range(8):
            here = col == first + m
            pivot = spread(cols[m][0], m)
            inverse = 1.0 / pivot
            pivots[tile] = jnp.where(sub == m, pivot, pivots[tile])
            cols[m][0] = jnp.where(sub > m, cols[m][0], 0.0)
            for n in range(m + 1, 8):
                ratio = spread(cols[n][0], m) * inverse
                cols[n] = [c - f * ratio for c, f in zip(cols[n], cols[m])]
            scaled = jnp.where(here, 1.0, spread(rows[tile], m)) * inverse
            for r in range(tile, 8):
                rows[r] = jnp.where(here, 0.0, rows[r]) - cols[m][r - tile] * scaled
    done = []
    for r in range(8):
        row = sub + 8 * r
        scale = lax.rsqrt(pivots[r])
        done.append(jnp.where(col < row, rows[r] * scale, jnp.where(col == row, scale, 0.0)))
    return jnp.concatenate(done, axis=0)


def diagonal_pair(packed):
    lane = lax.broadcasted_iota(jnp.int32, packed.shape, 1)
    first = lax.rem(lane, 2 * HALF) < HALF
    return jnp.concatenate([jnp.where(first, packed, 0.0), jnp.where(first, 0.0, packed)], axis=0)


def invert_factors(matrices):
    width = matrices[0].shape[0]
    count = width // HALF
    parts = range(0, width, HALF)
    grid = [
        [jnp.concatenate([m[i : i + HALF, j : j + HALF] for m in matrices], axis=1) for j in parts] for i in parts
    ]
    lane = lax.broadcasted_iota(jnp.int32, (HALF, 2 * HALF), 1)
    eye = (lax.broadcasted_iota(jnp.int32, lane.shape, 0) == lax.rem(lane, HALF)).astype(jnp.float32)
    none = jnp.zeros(lane.shape, jnp.float32)
    done = []
    for k in range(count):
        both = inverse_factor_pair([grid[k][k][8 * r : 8 * r + 8] for r in range(8)])
        row = jnp.concatenate([eye if j == k else grid[k][j] for j in range(count)], axis=1)
        panel = product(both, diagonal_pair(row), 1, 0)
        if k + 1 < count:
            corner, spread_panel = diagonal_pair(both), diagonal_pair(panel)
            for i in range(k + 1, count):
                below = product(product(grid[i][k], corner, 1, 1), spread_panel, 1, 0)
                grid[i][k] = none
                grid[i] = [grid[i][j] - below[:, 2 * HALF * j : 2 * HALF * (j + 1)] for j in range(count)]
        done.append([panel[:, 2 * HALF * j : 2 * HALF * (j + 1)] if j <= k else none for j in range(count)])
    return [
        jnp.concatenate(
            [jnp.concatenate([b[:, HALF * m : HALF * (m + 1)] for b in blocks], axis=1) for blocks in done], axis=0
        )
        for m in range(2)
    ]


def rotation_into(turns, r, cross, norm, right_is_there):
    width = cross.shape[0]
    norm_top = jnp.broadcast_to(jnp.sum(norm[0], axis=0, keepdims=True), (width, width)).T
    norm_low = jnp.sum(norm[1], axis=0, keepdims=True)
    coupling = 2.0 * cross[...] / (norm_top + norm_low + epsilon)
    cross[...] = coupling
    row = lax.broadcasted_iota(jnp.int32, (width, width), 0)
    eye = (row == lax.broadcasted_iota(jnp.int32, (width, width), 1)).astype(jnp.float32)
    top_inverse, low_inverse = invert_factors(
        [eye + product(coupling, coupling, 1, 1), eye + product(coupling, coupling, 0, 0)]
    )
    turns[r, 1, 0:width, :] = product(cross[...], low_inverse, 1, 1).astype(jnp.bfloat16)
    turns[r, 1, width:, :] = low_inverse.T.astype(jnp.bfloat16)
    right_is_there()
    turns[r, 0, 0:width, :] = top_inverse.T.astype(jnp.bfloat16)
    turns[r, 0, width:, :] = (-product(cross[...], top_inverse, 0, 1)).astype(jnp.bfloat16)


def own_ring_position():
    group, pair = lax.axis_index("group"), lax.axis_index("pair")
    return (group // 2) * 2 + lax.rem(pair, 2), lax.rem(group, 2)


def whole_kernel(
    dest, counts, top_out, low_out,
    read, slots, landed, passed, tops, lows, shadow, shadow_low, cross, norm, turns, shadow_turns,
    read_sem, send, recv, pass_send, copy_send, copy_recv, move_send, move_recv, after_send, after_recv,
    turn_send, turn_recv, top_send, top_recv, low_send, low_recv,
):
    rows, width = tops.shape[1:]
    chunks = rows // CHUNK
    y, core = own_ring_position()
    side = lax.rem(y, 2)
    column = lax.axis_index("pair") // 2
    even = core == 0
    pass_second, wanted, first_slot = choices(dest)

    def device(ahead, y, core):
        y = lax.rem(y + 4, 4)
        there = lax.rem(column + ahead + 16, 16)
        return {"group": (y // 2) * 2 + core, "pair": there * 2 + lax.rem(y, 2)}

    def part(i):
        return pl.ds(pl.multiple_of(i * CHUNK, CHUNK), CHUNK)

    def reading(i):
        return pltpu.make_async_copy(counts.at[part(i)], read.at[part(i)], read_sem.at[i])

    @pl.loop(0, chunks)
    def _(i):
        reading(i).start()

    partner = device(0, y, 1 - core)
    after = device(1, y, 0)
    base = y - side
    top_device = device(0, base + core, side)
    low_device = device(core, base + 1 - core, side)
    low_source = device(side - 1, base + core, 1 - side)

    barrier = pltpu.get_barrier_semaphore()
    others = [partner, low_device, low_source]
    others += [device(0, y + step, c) for step in (1, -1) for c in (0, 1)]
    others += [device(step, y, c) for step in (1, -1) for c in (0, 1)]
    for other in others:
        pl.semaphore_signal(barrier, inc=1, device_id=other)

    @pl.when(core != side)
    def _():
        pl.semaphore_signal(barrier, inc=1, device_id=top_device)
        pl.semaphore_wait(barrier, len(others) + 1)

    @pl.when(core == side)
    def _():
        pl.semaphore_wait(barrier, len(others))


    def away(slot, i):
        place = core if slot == 1 else 2 + core
        return pltpu.make_async_remote_copy(
            src_ref=slots.at[slot, part(i)],
            dst_ref=landed.at[place, part(i)],
            send_sem=send.at[slot, i],
            recv_sem=recv.at[place, i],
            device_id=device(0, y + (1 if slot == 1 else -1), side),
        )

    def across(i):
        return pltpu.make_async_remote_copy(
            src_ref=slots.at[0, part(i)],
            dst_ref=landed.at[core, part(i)],
            send_sem=send.at[0, i],
            recv_sem=recv.at[core, i],
            device_id=partner,
        )

    def stay(i):
        return pltpu.make_async_copy(slots.at[0, part(i)], landed.at[core, part(i)], recv.at[core, i])

    def onward(way, i):
        return pltpu.make_async_remote_copy(
            src_ref=passed.at[way, part(i)],
            dst_ref=landed.at[2 + way, part(i)],
            send_sem=pass_send.at[way, i],
            recv_sem=recv.at[2 + way, i],
            device_id=device(0, y + (1 if way == 0 else -1), core),
        )

    def arrival(place, i):
        here = landed.at[place, part(i)]
        pltpu.make_async_copy(here, here, recv.at[place, i]).wait()


    def copied(m, i):
        source = tops if m == 0 else lows
        return pltpu.make_async_remote_copy(
            src_ref=source.at[0, part(i)],
            dst_ref=shadow.at[m, part(i)],
            send_sem=copy_send.at[m, i],
            recv_sem=copy_recv.at[m, i],
            device_id=after,
        )

    def turned(k):
        r, half = ((0, 1), (0, 0), (1, 1))[k]
        return pltpu.make_async_remote_copy(
            src_ref=turns.at[r, half],
            dst_ref=shadow_turns.at[k],
            send_sem=turn_send.at[k],
            recv_sem=turn_recv.at[k],
            device_id=after,
        )

    def followed(i):
        return pltpu.make_async_remote_copy(
            src_ref=slots.at[0, part(i)],
            dst_ref=shadow_low.at[part(i)],
            send_sem=after_send.at[i],
            recv_sem=after_recv.at[i],
            device_id=after,
        )

    def move(r, i):
        return pltpu.make_async_remote_copy(
            src_ref=slots.at[r, part(i)],
            dst_ref=lows.at[r + 1, part(i)],
            send_sem=move_send.at[r, i],
            recv_sem=move_recv.at[r, i],
            device_id=partner,
        )

    def top_home(i):
        return pltpu.make_async_remote_copy(
            src_ref=tops.at[1, part(i)],
            dst_ref=top_out.at[part(i)],
            send_sem=top_send.at[i],
            recv_sem=top_recv.at[i],
            device_id=top_device,
        )

    def top_stays(i):
        return pltpu.make_async_copy(tops.at[1, part(i)], top_out.at[part(i)], top_recv.at[i])

    def low_home(i):
        return pltpu.make_async_remote_copy(
            src_ref=slots.at[ROUNDS - 1, part(i)],
            dst_ref=low_out.at[part(i)],
            send_sem=low_send.at[i],
            recv_sem=low_recv.at[i],
            device_id=low_device,
        )


    def gather_sums(i, sums):
        reading(i).wait()
        values = read[part(i), :].astype(jnp.float32).reshape(CHUNK // 8, 8, 2 * width)
        return sums[0] + jnp.sum(values, axis=0), sums[1] + jnp.sum(values * values, axis=0)

    nothing = jnp.zeros((8, 2 * width), jnp.float32)
    sums = lax.fori_loop(0, chunks, gather_sums, (nothing, nothing))
    total, squares = (jnp.sum(one, axis=0, keepdims=True) for one in sums)
    mean = total * (1.0 / rows)
    whole = total.astype(jnp.int32)
    spread_of = (rows * squares.astype(jnp.int32) - whole * whole).astype(jnp.float32)
    factor = 1.0 / jnp.sqrt(spread_of * (1.0 / (rows * rows)) + epsilon)

    @pl.loop(0, chunks)
    def _(i):
        scaled = ((read[part(i), :].astype(jnp.float32) - mean) * factor).astype(jnp.bfloat16)
        for slot in range(3):
            slots[slot, part(i), :] = jnp.where(first_slot == slot, scaled[:, :width], scaled[:, width:])

        @pl.when(i < AHEAD)
        def _():
            away(1, i).start()
            away(2, i).start()

        @pl.when(core == side)
        def _():
            stay(i).start()

        @pl.when(core != side)
        def _():
            across(i).start()

    def add_products(blocks):
        cross[...] += lax.dot_general(
            *blocks, (((0,), (0,)), ((), ())), preferred_element_type=jnp.float32
        )
        for m, block in enumerate(blocks):
            wide = block.astype(jnp.float32)
            norm[m] += jnp.sum((wide * wide).reshape(CHUNK // 8, 8, width), axis=0)

    def clear_products():
        cross[...] = jnp.zeros_like(cross)
        norm[...] = jnp.zeros_like(norm)

    clear_products()

    @pl.loop(0, chunks)
    def _(i):
        for way in range(2):
            for place in (2 * way, 2 * way + 1):
                arrival(place, i)

            @pl.when(core != side)
            def _():
                first, second = landed[2 * way, part(i)], landed[2 * way + 1, part(i)]
                passed[way, part(i)] = jnp.where(pass_second[way] > 0, second, first)
                onward(way, i).start()

        @pl.when(i < chunks - AHEAD)
        def _():
            away(1, i + AHEAD).start()
            away(2, i + AHEAD).start()

        blocks = []
        for which, target in zip(wanted, (tops, lows)):
            lower = jnp.where(which == 0, landed[0, part(i)], landed[1, part(i)])
            upper = jnp.where(which == 2, landed[2, part(i)], landed[3, part(i)])
            block = jnp.where(which < 2, lower, upper)
            target[0, part(i), :] = block
            blocks.append(block)

        @pl.when(jnp.logical_not(even))
        def _():
            copied(0, i).start()
            copied(1, i).start()

        add_products(blocks)

    def matmul(left, right, turn):
        joined = jnp.concatenate([left, right], axis=1)
        return jnp.dot(joined, turn, preferred_element_type=jnp.float32).astype(jnp.bfloat16)

    @pl.loop(0, chunks)
    def _(i):
        for slot in (1, 2):
            away(slot, i).wait_send()

        @pl.when(core != side)
        def _():
            across(i).wait_send()

    @pl.loop(0, ROUNDS)
    def _(r):
        here = jnp.minimum(r, 1)

        @pl.when(r > 0)
        def _():
            clear_products()

            @pl.when(even & (r == 1))
            def _():
                turned(0).wait_recv()

            @pl.when(even & (r == 2))
            def _():
                turned(1).wait_recv()

                @pl.loop(0, chunks)
                def _(i):
                    shadow[0, part(i)] = matmul(shadow[0, part(i)], shadow[1, part(i)], shadow_turns[1])

                turned(2).wait_recv()

            @pl.loop(0, chunks)
            def _(i):
                @pl.when(jnp.logical_not(even))
                def _():
                    move(r - 1, i).wait_recv()

                @pl.when(even & (r == 1))
                def _():
                    copied(0, i).wait_recv()
                    copied(1, i).wait_recv()
                    lows[1, part(i), :] = matmul(shadow[0, part(i)], shadow[1, part(i)], shadow_turns[0])

                @pl.when(even & (r == 2))
                def _():
                    followed(i).wait_recv()
                    lows[2, part(i), :] = matmul(shadow[0, part(i)], shadow_low[part(i)], shadow_turns[2])

                add_products([tops[1, part(i), :], lows[r, part(i), :]])

        def send_right():
            @pl.when(jnp.logical_not(even) & (r == 0))
            def _():
                turned(0).start()

            @pl.when(jnp.logical_not(even) & (r == 1))
            def _():
                turned(2).start()

        rotation_into(turns, r, cross, norm, send_right)

        @pl.when(jnp.logical_not(even) & (r == 0))
        def _():
            turned(1).start()

        @pl.loop(0, chunks)
        def _(i):
            top, low = tops[here, part(i), :], lows[r, part(i), :]

            @pl.when(even | (r == ROUNDS - 1))
            def _():
                slots[r, part(i), :] = matmul(top, low, turns[r, 1])

            @pl.when(even & (r < ROUNDS - 1))
            def _():
                move(r, i).start()

            @pl.when(even & (r == 0))
            def _():
                followed(i).start()

            @pl.when(r == ROUNDS - 1)
            def _():
                low_home(i).start()

            tops[1, part(i), :] = matmul(top, low, turns[r, 0])

            @pl.when((r == ROUNDS - 1) & (core != side))
            def _():
                top_home(i).start()

            @pl.when((r == ROUNDS - 1) & (core == side))
            def _():
                top_stays(i).start()

    @pl.when(jnp.logical_not(even))
    def _():
        for k in range(3):
            turned(k).wait_send()

    @pl.loop(0, chunks)
    def _(i):
        @pl.when(core != side)
        def _():
            for way in range(2):
                onward(way, i).wait_send()
            top_home(i).wait()

        @pl.when(core == side)
        def _():
            top_stays(i).wait()

        @pl.when(even)
        def _():
            followed(i).wait_send()
            for r in range(ROUNDS - 1):
                move(r, i).wait_send()

        @pl.when(jnp.logical_not(even))
        def _():
            copied(0, i).wait_send()
            copied(1, i).wait_send()

        low_home(i).wait()


def play(dest, counts):
    rows, width = counts.shape[0], counts.shape[1] // 2
    chunks = rows // CHUNK
    anywhere = pl.BlockSpec(memory_space=pl.ANY)

    def blocks(count):
        return pltpu.VMEM((count, rows, width), jnp.bfloat16)

    def dma(*shape):
        return pltpu.SemaphoreType.DMA(shape)

    return pl.pallas_call(
        whole_kernel,
        out_shape=[jax.ShapeDtypeStruct((rows, width), jnp.bfloat16)] * 2,
        in_specs=[pl.BlockSpec(memory_space=pltpu.SMEM), anywhere],
        out_specs=[anywhere, anywhere],
        scratch_shapes=[
            pltpu.VMEM((rows, 2 * width), jnp.int32),
            blocks(3),
            blocks(4),
            blocks(2),
            blocks(2),
            blocks(ROUNDS),
            blocks(2),
            pltpu.VMEM((rows, width), jnp.bfloat16),
            pltpu.VMEM((width, width), jnp.float32),
            pltpu.VMEM((2, 8, width), jnp.float32),
            pltpu.VMEM((ROUNDS, 2, 2 * width, width), jnp.bfloat16),
            pltpu.VMEM((3, 2 * width, width), jnp.bfloat16),
            dma(chunks),
            dma(3, chunks),
            dma(4, chunks),
            dma(2, chunks),
            dma(2, chunks),
            dma(2, chunks),
            dma(ROUNDS - 1, chunks),
            dma(ROUNDS - 1, chunks),
            dma(chunks),
            dma(chunks),
            dma(3),
            dma(3),
            dma(chunks),
            dma(chunks),
            dma(chunks),
            dma(chunks),
        ],
        compiler_params=pltpu.CompilerParams(
            collective_id=0, has_side_effects=True, vmem_limit_bytes=49 * 2**20
        ),
    )(dest, counts)


def routed(dest, group, pair, side):
    chip = (group // 2) * 2 + lax.rem(pair, 2)
    distance, other = (lax.rem(dest[(group * 32 + pair) * 2 + k] - chip + 4, 4) for k in (side, 1 - side))
    slot = jnp.where(distance == 2, jnp.where(other == 1, 2, 1), jnp.where(distance == 3, 2, distance))
    return distance, slot


def choices(dest):
    y, core = own_ring_position()
    group, own_pair = lax.axis_index("group"), lax.axis_index("pair")
    pair = (own_pair // 2) * 2 + core

    def passing(chip, slot):
        distance, used = routed(dest, (chip // 2) * 2 + 1, pair, 0)
        other, other_used = routed(dest, (chip // 2) * 2 + 1, pair, 1)
        far = ((distance == 2) & (used == slot)) | ((other == 2) & (other_used == slot))
        return far.astype(jnp.int32)

    def landing(side):
        found = jnp.int32(0)
        for source in range(4):
            distance, slot = routed(dest, source, pair, side)
            origin = source % 2
            near = jnp.where(distance == 1, origin, 2 + origin)
            place = jnp.where(lax.rem(distance, 2) == 1, near, jnp.where(distance == 0, origin, 1 + slot))
            found = found + jnp.where(dest[(source * 32 + pair) * 2 + side] == y, place, 0)
        return found

    first = routed(dest, group, own_pair, 0)[1]
    return (
        (passing(lax.rem(y + 3, 4), 1), passing(lax.rem(y + 1, 4), 2)),
        (landing(0), landing(1)),
        first,
    )


def body(genotypes, dest_group):
    top, low = play(dest_group, genotypes)
    return jnp.concatenate([top, low], axis=1)


def solution(mesh):
    in_specs = (P(None, ("group", "pair")), P())
    out_specs = P(None, ("group", "pair"))
    return jax.shard_map(body, mesh=mesh, in_specs=in_specs, out_specs=out_specs, check_vma=False)
```
